512 devices in a mesh: cuts: 32 (over x_hi, y, core), slab: 16 (over z, x_lo).
Axes of the slice: x: 4 (x_hi: 2, x_lo: 2; x = x_hi * 2 + x_lo), y: 8, z: 8, core: 2. Of those that a mesh axis runs over, the one named last changes fastest.
Arguments:
- orbitals: bfloat16 [1024, 64, 4096], P('cuts', 'slab'), may hold values from -0.25 to 0.25
- occupation: int32 [32, 32], P('cuts'), may hold values from 0 to 8
- state_counts: int32 [32], P('cuts'), may hold values from 8 to 32
- ion_charge: float32 [64, 4096], P('slab'), may hold values from 0.2 to 1.2, as said below
Outputs:
- potential: float32 [64, 4096], P('slab')
- kinetic: float32 [64, 4096], P('slab', 'cuts')
The draws below stay inside these ranges and needn't reach their ends.
Inputs may be any that keep to these rules, and one draw needn't show every extreme that they name: `ion_charge`: the ionic charge is positive.
All inputs are finite; a program needn't handle non-finite values.
Results may differ from the reference program's by a relative error of at most 0.0003.
Values may be sent and summed in bfloat16 or wider, within the bound.
A program may use at most 64 MiB of HBM per device.

```python
import jax
import jax.numpy as jnp
from jax import lax

STATES = 32
NX = 64
LEVELS = 3
CYCLES = 2
COARSE_SWEEPS = 4
OCC_DEN = 8
GROUPS = 32
STATES_ALL = 1024
NZ = 64
PLANE = 4096


def draw_ion_charge(key, part):
    rough_part = jax.random.uniform(key, (NZ, NX * NX), jnp.float32)
    return 0.35 + 0.7 * rough_part


def touch_ends(entries, rng, smallest, largest):
    spot = [jax.random.randint(jax.random.fold_in(rng, axis), (), 0, length) for axis, length in enumerate(entries.shape)]
    main_axis = entries.shape.index(max(entries.shape))
    beside = spot[:main_axis] + [(spot[main_axis] + 1) % entries.shape[main_axis]] + spot[main_axis + 1:]
    return entries.at[tuple(spot)].set(smallest).at[tuple(beside)].set(largest)


def shard_levels(rng, shape, split, smallest, high):
    loudness = 1.0
    for dim, shards_of in split:
        steps = jax.random.uniform(jax.random.fold_in(jax.random.fold_in(rng, 6), dim), (shards_of,), jnp.float32, smallest / len(split), high / len(split))
        loudness = loudness * jnp.repeat(jnp.exp(steps), shape[dim] // shards_of).reshape((-1,) + (1,) * (len(shape) - 1 - dim))
    return loudness


def gaussian(stream_key, extent, scale, reach, pieces=(), kind=jnp.bfloat16):
    values = jax.random.normal(stream_key, extent, jnp.float32) * scale
    if len(pieces) > 0:
        values = shard_levels(stream_key, extent, pieces, -0.22, 0.18) * values
    return jnp.clip(values, min=-reach, max=reach).astype(kind)


def setup_inputs(seed: int = 0) -> dict:
    seeds = jax.random.split(jax.random.key(seed), 5)
    return {
        "orbitals": gaussian(seeds[0], (STATES_ALL, NZ, PLANE), ((2.0 / STATES_ALL) ** 0.5), 0.25, ((0, 32), (1, 16))),
        "occupation": touch_ends(jax.random.randint(seeds[1], (GROUPS, STATES), 0, OCC_DEN + 1), jax.random.fold_in(seeds[1], 1), 0, OCC_DEN).astype(jnp.int32),
        "state_counts": touch_ends(jax.random.randint(seeds[2], (GROUPS,), STATES // 4, STATES + 1), jax.random.fold_in(seeds[2], 1), STATES // 4, STATES).astype(jnp.int32),
        "ion_charge": draw_ion_charge(jax.random.fold_in(seeds[4], 71), 0),
    }


OMEGA = 0.8
COUPLING = 4.0


def take_next(values, offset):
    padding = [(0, 0)] * (values.ndim - 1) + [(0, offset)]
    return jnp.pad(values[..., offset:], padding)


def take_prev(values, offset):
    padding = [(0, 0)] * (values.ndim - 1) + [(offset, 0)]
    return jnp.pad(values[..., :-offset], padding)


def x_neighbours(values, side_cells):
    column = jnp.arange(values.shape[-1]) % side_cells
    next_cell = jnp.where(column != side_cells - 1, take_next(values, 1), 0.0)
    prev_cell = jnp.where(column != 0, take_prev(values, 1), 0.0)
    return next_cell, prev_cell


def plane_sum(values, side_cells):
    next_cell, prev_cell = x_neighbours(values, side_cells)
    return next_cell + prev_cell + take_next(values, side_cells) + take_prev(values, side_cells)


def stencil(iterate, padded, side_cells, degree):
    return (6.0 * iterate - plane_sum(iterate, side_cells) - padded[2:] - padded[:-2]) * (0.25 ** degree)


def smooth(iterate, forcing, padded, side_cells, degree):
    return iterate + (OMEGA * 4.0 ** degree / 6.0) * (forcing - stencil(iterate, padded, side_cells, degree))


def restrict(residual, side_cells):
    planes = residual.shape[0]
    half_cells = side_cells // 2
    blocks = residual.reshape(planes // 2, 2, half_cells, 2, half_cells, 2)
    return jnp.mean(blocks, axis=(1, 3, 5)).reshape(planes // 2, half_cells * half_cells)


def prolong(coarse, half_cells):
    planes = coarse.shape[0]
    spread = jnp.broadcast_to(coarse.reshape(planes, 1, half_cells, 1, half_cells, 1), (planes, 2, half_cells, 2, half_cells, 2))
    return spread.reshape(2 * planes, 4 * half_cells * half_cells)


def pad_planes(iterate):
    return jnp.pad(iterate, ((1, 1), (0, 0)))


def vcycle(degree, iterate, forcing, side_cells, surround):
    if degree == LEVELS - 1:
        for sweep_index in range(COARSE_SWEEPS):
            iterate = smooth(iterate, forcing, surround(iterate), side_cells, degree)
        return iterate
    iterate = smooth(iterate, forcing, surround(iterate), side_cells, degree)
    residual = forcing - stencil(iterate, surround(iterate), side_cells, degree)
    coarse_forcing = restrict(residual, side_cells)
    correction = vcycle(degree + 1, jnp.zeros_like(coarse_forcing), coarse_forcing, side_cells // 2, surround)
    iterate = iterate + prolong(correction, side_cells // 2)
    return smooth(iterate, forcing, surround(iterate), side_cells, degree)


def live_weights(occupation_row, live_count):
    ranks = jnp.arange(occupation_row.shape[0])
    return jnp.where(ranks < live_count, occupation_row.astype(jnp.float32) / OCC_DEN, 0.0)


def orbital_terms(padded, weights, side_cells):
    values = padded.astype(jnp.float32)
    interior = values[:, 1:-1]
    next_cell, prev_cell = x_neighbours(interior, side_cells)
    slope_x = (next_cell - prev_cell) * 0.5
    slope_y = (take_next(interior, side_cells) - take_prev(interior, side_cells)) * 0.5
    slope_z = (values[:, 2:] - values[:, :-2]) * 0.5
    density = jnp.einsum("s,szf->zf", weights, interior * interior, precision=lax.Precision.HIGHEST)
    squares = slope_x * slope_x + slope_y * slope_y + slope_z * slope_z
    kinetic = 0.5 * jnp.einsum("s,szf->zf", weights, squares, precision=lax.Precision.HIGHEST)
    return density, kinetic


def reference(orbitals, occupation, state_counts, ion_charge):
    orbital_blocks = orbitals.reshape(GROUPS, STATES, NZ, PLANE)

    def accumulate(totals, block_items):
        orbital_block, occupation_row, live_count = block_items
        padded = jnp.pad(orbital_block, ((0, 0), (1, 1), (0, 0)))
        density, kinetic = orbital_terms(padded, live_weights(occupation_row, live_count), NX)
        return (totals[0] + density, totals[1] + kinetic), None

    zero_field = jnp.zeros((NZ, PLANE), jnp.float32)
    (density, kinetic), unused = lax.scan(accumulate, (zero_field, zero_field), (orbital_blocks, occupation, state_counts))
    forcing = COUPLING * (density - ion_charge)
    potential = jnp.zeros_like(forcing)
    for repeat in range(CYCLES):
        potential = vcycle(0, potential, forcing, NX, pad_planes)
    return potential, kinetic
```

```python
import functools

import jax
import jax.numpy as jnp
from jax import lax
from jax.experimental import pallas as pl
from jax.experimental.pallas import tpu as pltpu
from jax.sharding import PartitionSpec as P

MESH = pl.DeviceIdType.MESH
HIGHEST = lax.Precision.HIGHEST
NX = 64
OCC_DEN = 8
OMEGA = 0.8
COUPLING = 4.0
STEP = OMEGA / 6.0
GAIN0, GAIN1, GAIN2 = STEP, 4.0 * STEP, 16.0 * STEP


def iota(shape, axis):
    return lax.broadcasted_iota(jnp.int32, shape, axis)


def fine_cross(v):
    shape = v.shape
    lane, row = iota(shape, 2), iota(shape, 1)
    column = lane & 63
    west = jnp.where(column == 0, 0.0, pltpu.roll(v, 1, 2))
    east = jnp.where(column == 63, 0.0, pltpu.roll(v, 127, 2))
    odd = lane >= 64
    before = jnp.where(row == 0, 0.0, pltpu.roll(v, 1, 1))
    after = jnp.where(row == 31, 0.0, pltpu.roll(v, 31, 1))
    return west + east + pltpu.roll(v + jnp.where(odd, before, after), 64, 2)


def mid_cross(v):
    shape = v.shape
    lane, row = iota(shape, 2), iota(shape, 1)
    along = pltpu.roll(v, 1, 2) + pltpu.roll(v, 127, 2)
    before = jnp.where(row == 0, 0.0, pltpu.roll(v, 1, 1))
    after = jnp.where(row == 31, 0.0, pltpu.roll(v, 31, 1))
    return jnp.where(lane < 32, along + before + after, 0.0)


def relax(v, cross):
    inner = v[1:-1]
    return (1.0 - OMEGA) * inner + STEP * (cross(inner) + v[2:] + v[:-2])


def inside(v, first, planes):
    plane = iota(v.shape, 0) + first
    return jnp.where((plane >= 0) & (plane < planes), v, 0.0)


def flat_dot(v, m):
    n = v.shape[0]
    out = jnp.dot(v.reshape(n * v.shape[1], 128), m, precision=HIGHEST, preferred_element_type=jnp.float32)
    return out.reshape(n, v.shape[1], 128)


def restrict_fine(v):
    n = v.shape[0]
    pairs = v.reshape(n // 2, 2, 32, 128)
    lane, x = iota((128, 128), 0), iota((128, 128), 1)
    average = jnp.where(((lane & 63) >> 1) == x, 0.125, 0.0)
    return flat_dot(pairs[:, 0] + pairs[:, 1], average)


def prolong_fine(v):
    n = v.shape[0]
    x, lane = iota((128, 128), 0), iota((128, 128), 1)
    spread = flat_dot(v, jnp.where(((lane & 63) >> 1) == x, 1.0, 0.0))
    return jnp.broadcast_to(spread[:, None], (n, 2, 32, 128)).reshape(2 * n, 32, 128)


def own_group(shape):
    return ((iota(shape, len(shape) - 2) >> 1) & 7) == (iota(shape, len(shape) - 1) >> 4)


def restrict_mid(pair):
    x, lane = iota((128, 128), 0), iota((128, 128), 1)
    average = jnp.where(((lane & 15) == (x >> 1)) & (x < 32), 0.125, 0.0)
    both = jnp.dot(pair[0] + pair[1], average, precision=HIGHEST, preferred_element_type=jnp.float32)
    both = jnp.where(own_group(both.shape), both, 0.0)
    upper = jnp.sum(both[:16], axis=0, keepdims=True)
    lower = jnp.sum(both[16:], axis=0, keepdims=True)
    row = iota((8, 128), 0)
    return jnp.where(row == 0, upper, jnp.where(row == 1, lower, 0.0))


def prolong_mid(v):
    n = v.shape[0]
    rows = jnp.concatenate(
        [jnp.broadcast_to(v[:, 0:1], (n, 16, 128)), jnp.broadcast_to(v[:, 1:2], (n, 16, 128))], axis=1
    )
    rows = jnp.where(own_group(rows.shape), rows, 0.0)
    lane, x = iota((128, 128), 0), iota((128, 128), 1)
    spread = flat_dot(rows, jnp.where(((lane & 15) == (x >> 1)) & (x < 32), 1.0, 0.0))
    return jnp.broadcast_to(spread[:, None], (n, 2, 32, 128)).reshape(2 * n, 32, 128)


def coarse_solve(source):
    shape = source.shape
    lane, row = iota(shape, 2), iota(shape, 1)
    column, group = lane & 15, lane >> 4
    zero = jnp.zeros((1, *shape[1:]), jnp.float32)
    gained = GAIN2 * source
    v = gained
    for unused in range(3):
        west = jnp.where(column == 0, 0.0, pltpu.roll(v, 1, 2))
        east = jnp.where(column == 15, 0.0, pltpu.roll(v, 127, 2))
        back, on = pltpu.roll(v, 16, 2), pltpu.roll(v, 112, 2)
        before = jnp.where(group == 0, pltpu.roll(back, 1, 1), back)
        after = jnp.where(group == 7, pltpu.roll(on, 7, 1), on)
        plane = jnp.where(row < 2, west + east + before + after, 0.0)
        below = jnp.concatenate([zero, v[:-1]], axis=0)
        above = jnp.concatenate([v[1:], zero], axis=0)
        v = (1.0 - OMEGA) * v + STEP * (plane + below + above) + gained
    return v


def kernel(
    blocks, slabs,
    orb_ref, occ_ref, count_ref, ion_ref,
    pot_ref, kin_ref,
    dens, dens_in, field, field_below, field_above, rims, kin, kin_in,
    mids, coarse, coarse_again, padded, fine,
    send_sem, recv_sem,
):
    me, slab = lax.axis_index("cuts"), lax.axis_index("slab")
    planes = 4 * slabs

    def cut_at(r):
        return {"cuts": lax.rem(me + r, blocks)}

    def slab_at(r):
        return {"slab": lax.rem(slab + r + slabs, slabs)}

    barrier = pltpu.get_barrier_semaphore()

    @pl.loop(1, blocks)
    def _(r):
        pl.semaphore_signal(barrier, inc=1, device_id=cut_at(r), device_id_type=MESH)

    @pl.loop(1, slabs)
    def _(r):
        pl.semaphore_signal(barrier, inc=1, device_id=slab_at(r), device_id_type=MESH)

    def copy(stage, src, dst, device):
        return pltpu.make_async_remote_copy(
            src_ref=src, dst_ref=dst, send_sem=send_sem.at[stage], recv_sem=recv_sem.at[stage],
            device_id=device, device_id_type=MESH,
        )

    square = (32, 32)
    column = jnp.sum(
        jnp.where(
            iota(square, 0) == iota(square, 1),
            jnp.broadcast_to(occ_ref[...].astype(jnp.float32), square), 0.0,
        ),
        axis=1, keepdims=True,
    ) * (1.0 / OCC_DEN)
    live = iota((32, 128), 0) < count_ref[0]
    weight = jnp.where(live, jnp.broadcast_to(column, (32, 128)), 0.0)

    def tile(z, c):
        return orb_ref[z, :, pl.ds(pl.multiple_of(c * 128, 128), 128)].astype(jnp.float32)

    @pl.loop(0, blocks)
    def _(c):
        rows = []
        for z in range(4):
            p = tile(z, c)
            rows.append(jnp.sum(weight * (p * p), axis=0, keepdims=True))
        dens[c] = jnp.concatenate(rows, axis=0)

    pl.semaphore_wait(barrier, blocks + slabs - 2)

    @pl.loop(1, blocks)
    def _(r):
        copy(0, dens.at[lax.rem(me + r, blocks)], dens_in.at[r], cut_at(r)).start()

    up, down = slab_at(1), slab_at(-1)
    rim_up = copy(1, orb_ref.at[3], rims.at[0], up)
    rim_down = copy(2, orb_ref.at[0], rims.at[1], down)
    rim_up.start()
    rim_down.start()
    dens_in[0] = dens[me]

    lane = iota((32, 128), 1)
    x = lane & 63
    odd = lane >= 64

    @pl.loop(0, blocks)
    def _(c):
        left = jnp.where(c > 0, 1.0, 0.0)
        right = jnp.where(c < blocks - 1, 1.0, 0.0)
        ps = [tile(z, c) for z in range(4)]
        rows = []
        for z in range(4):
            p = ps[z]
            along = jnp.where(x == 0, 0.0, p) - jnp.where(x == 1, 0.0, pltpu.roll(p, 2, 1))
            total = pltpu.roll(weight * (along * along), 127, 1)
            back = p - left * tile(z, lax.max(c - 1, 0))
            on = right * tile(z, lax.min(c + 1, blocks - 1)) - p
            across = jnp.where(odd, back, on)
            total += pltpu.roll(weight * (across * across), 64, 1)
            if z in (1, 2):
                steep = ps[z + 1] - ps[z - 1]
                total += weight * (steep * steep)
            rows.append(jnp.sum(total, axis=0, keepdims=True) * 0.125)
        kin[c] = jnp.concatenate(rows, axis=0)

    copy(0, dens_in.at[pl.ds(1, blocks - 1)], dens_in.at[pl.ds(1, blocks - 1)], cut_at(1)).wait_recv()
    charge = ion_ref[:, pl.ds(pl.multiple_of(me * 128, 128), 128)]
    field[me] = COUPLING * (jnp.sum(dens_in[...], axis=0) - charge)

    @pl.loop(1, blocks)
    def _(r):
        copy(3, field.at[me], field.at[me], cut_at(r)).start()

    gathered = field.at[pl.ds(0, blocks - 1)]
    copy(3, gathered, gathered, cut_at(1)).wait_recv()
    field_up = copy(4, field, field_below, up)
    field_down = copy(5, field, field_above, down)
    field_up.start()
    field_down.start()
    field_up.wait_recv()
    field_down.wait_recv()

    for z in range(3):
        fine[z] = field_below[:, z + 1, :]
        fine[z + 7] = field_above[:, z, :]
    for z in range(4):
        fine[z + 3] = field[:, z, :]
    first = 4 * slab
    forcing = inside(fine[...], first - 3, planes)
    left1 = inside(relax(forcing, fine_cross), first - 2, planes)
    left2 = inside(relax(left1, fine_cross), first - 1, planes)
    left3 = relax(left2, fine_cross)
    direct = GAIN0 * (forcing[3:7] + left1[2:6] + left2[1:5] + left3)
    source = restrict_fine(left1)
    again = restrict_fine(left3)
    mids[3] = (
        source[1] + pltpu.roll(source[2], 32, 1) + pltpu.roll(again[0], 64, 1) + pltpu.roll(again[1], 96, 1)
    )
    coarse[slab] = restrict_mid(relax(source, mid_cross))
    for away in (1, -1, 2, -2, 3, -3):
        copy(6, mids.at[3], mids.at[3 - away], slab_at(away)).start()

    @pl.loop(1, slabs)
    def _(r):
        copy(7, coarse.at[slab], coarse.at[slab], slab_at(r)).start()

    rim_up.wait_recv()
    rim_down.wait_recv()
    has_below = jnp.where(slab > 0, 1.0, 0.0)
    has_above = jnp.where(slab < slabs - 1, 1.0, 0.0)
    row4 = iota((4, 128), 0)

    @pl.loop(0, blocks)
    def _(c):
        at = pl.ds(pl.multiple_of(c * 128, 128), 128)
        low = tile(1, c) - has_below * rims[0, :, at].astype(jnp.float32)
        high = has_above * rims[1, :, at].astype(jnp.float32) - tile(2, c)
        low = jnp.sum(weight * (low * low), axis=0, keepdims=True) * 0.125
        high = jnp.sum(weight * (high * high), axis=0, keepdims=True) * 0.125
        kin[c] += jnp.where(row4 == 0, low, jnp.where(row4 == 3, high, 0.0))

    @pl.loop(1, blocks)
    def _(r):
        copy(8, kin.at[lax.rem(me + r, blocks)], kin_in.at[r], cut_at(r)).start()

    kin_in[0] = kin[me]

    all_but_one = coarse.at[pl.ds(0, slabs - 1)]
    copy(7, all_but_one, all_but_one, up).wait_recv()
    padded[pl.ds(0, 3)] = jnp.zeros((3, 8, 128), jnp.float32)
    padded[pl.ds(slabs + 3, 3)] = jnp.zeros((3, 8, 128), jnp.float32)
    padded[pl.ds(3, slabs)] = coarse_solve(coarse[...])
    lifted = prolong_mid(padded[pl.ds(slab, 7)])
    copy(6, mids.at[pl.ds(0, 6)], mids.at[pl.ds(0, 6)], up).wait_recv()
    near = mids[...]
    use = iota((7, 32, 128), 2) < 32
    even = jnp.where(use, near, 0.0)
    uneven = jnp.where(use, pltpu.roll(near, 96, 2), 0.0)
    even_again = jnp.where(use, pltpu.roll(near, 64, 2), 0.0)[2:5]
    uneven_again = jnp.where(use, pltpu.roll(near, 32, 2), 0.0)[2:5]
    mid = 2 * slab
    source = jnp.concatenate([even[:, None], uneven[:, None]], axis=1).reshape(14, 32, 128)
    source = inside(source, mid - 6, 2 * slabs)
    again = jnp.concatenate([even_again[:, None], uneven_again[:, None]], axis=1).reshape(6, 32, 128)
    guess = GAIN1 * source[1:13] + lifted[1:13]
    error = inside(relax(guess, mid_cross) + GAIN1 * source[2:12], mid - 4, 2 * slabs)
    spread = prolong_fine(error)[1:19]
    back1 = inside(relax(spread, fine_cross), first - 6, planes)
    back2 = inside(relax(back1, fine_cross), first - 5, planes)
    back3 = relax(back2, fine_cross)
    direct += back3[4:8]
    source = again - restrict_fine((back2[1:13] - back3) * (1.0 / GAIN0))
    source = inside(source, mid - 2, 2 * slabs)

    coarse_again[slab] = restrict_mid(relax(source[1:5], mid_cross))

    @pl.loop(1, slabs)
    def _(r):
        copy(9, coarse_again.at[slab], coarse_again.at[slab], slab_at(r)).start()

    all_but_one = coarse_again.at[pl.ds(0, slabs - 1)]
    copy(9, all_but_one, all_but_one, up).wait_recv()
    padded[pl.ds(3, slabs)] = coarse_solve(coarse_again[...])
    lifted = prolong_mid(padded[pl.ds(slab + 2, 3)])
    guess = GAIN1 * source + lifted
    error = inside(relax(guess, mid_cross) + GAIN1 * source[1:5], mid - 1, 2 * slabs)
    pot_ref[...] = direct + relax(prolong_fine(error)[1:7], fine_cross)

    copy(8, kin_in.at[pl.ds(1, blocks - 1)], kin_in.at[pl.ds(1, blocks - 1)], cut_at(1)).wait_recv()
    kin_ref[...] = jnp.sum(kin_in[...], axis=0)

    copy(0, dens_in.at[pl.ds(1, blocks - 1)], dens_in.at[pl.ds(1, blocks - 1)], cut_at(1)).wait_send()
    rim_up.wait_send()
    rim_down.wait_send()
    copy(3, gathered, gathered, cut_at(1)).wait_send()
    field_up.wait_send()
    field_down.wait_send()
    copy(6, mids.at[pl.ds(0, 6)], mids.at[pl.ds(0, 6)], up).wait_send()
    copy(7, all_but_one, all_but_one, up).wait_send()
    copy(8, kin_in.at[pl.ds(1, blocks - 1)], kin_in.at[pl.ds(1, blocks - 1)], cut_at(1)).wait_send()
    copy(9, all_but_one, all_but_one, up).wait_send()


def solution(mesh):
    blocks, slabs = mesh.shape["cuts"], mesh.shape["slab"]

    def shards(orbitals, occupation, state_counts, ion_charge):
        f32 = jnp.float32
        by_plane = jnp.transpose(orbitals, (1, 0, 2))
        vmem = pl.BlockSpec(memory_space=pltpu.VMEM)
        smem = pl.BlockSpec(memory_space=pltpu.SMEM)
        potential, kinetic = pl.pallas_call(
            functools.partial(kernel, blocks, slabs),
            out_shape=(jax.ShapeDtypeStruct((4, 32, 128), f32), jax.ShapeDtypeStruct((4, 128), f32)),
            in_specs=[vmem, vmem, smem, vmem],
            out_specs=(vmem, vmem),
            scratch_shapes=[
                pltpu.VMEM((blocks, 4, 128), f32),
                pltpu.VMEM((blocks, 4, 128), f32),
                pltpu.VMEM((blocks, 4, 128), f32),
                pltpu.VMEM((blocks, 4, 128), f32),
                pltpu.VMEM((blocks, 4, 128), f32),
                pltpu.VMEM((2, 32, 4096), jnp.bfloat16),
                pltpu.VMEM((blocks, 4, 128), f32),
                pltpu.VMEM((blocks, 4, 128), f32),
                pltpu.VMEM((7, 32, 128), f32),
                pltpu.VMEM((slabs, 8, 128), f32),
                pltpu.VMEM((slabs, 8, 128), f32),
                pltpu.VMEM((slabs + 6, 8, 128), f32),
                pltpu.VMEM((10, 32, 128), f32),
                pltpu.SemaphoreType.DMA((10,)),
                pltpu.SemaphoreType.DMA((10,)),
            ],
            compiler_params=pltpu.CompilerParams(collective_id=0, has_side_effects=True),
        )(by_plane, occupation, state_counts, ion_charge)
        return potential.reshape(4, 4096), kinetic

    return jax.shard_map(
        shards,
        mesh=mesh,
        in_specs=(P("cuts", "slab", None), P("cuts", None), P("cuts"), P("slab", None)),
        out_specs=(P("slab", None), P("slab", "cuts")),
        check_vma=False,
    )
```

```python
import functools

import jax
import jax.numpy as jnp
from jax import lax
from jax.experimental import pallas as pl
from jax.experimental.pallas import tpu as pltpu
from jax.sharding import PartitionSpec as P

MESH = pl.DeviceIdType.MESH
HIGHEST = lax.Precision.HIGHEST
NX = 64
OCC_DEN = 8
OMEGA = 0.8
COUPLING = 4.0
STEP = OMEGA / 6.0
GAIN0, GAIN1, GAIN2 = STEP, 4.0 * STEP, 16.0 * STEP


def iota(shape, axis):
    return lax.broadcasted_iota(jnp.int32, shape, axis)


def fine_cross(v):
    shape = v.shape
    lane, row = iota(shape, 2), iota(shape, 1)
    column = lane & 63
    west = jnp.where(column == 0, 0.0, pltpu.roll(v, 1, 2))
    east = jnp.where(column == 63, 0.0, pltpu.roll(v, 127, 2))
    odd = lane >= 64
    before = jnp.where(row == 0, 0.0, pltpu.roll(v, 1, 1))
    after = jnp.where(row == 31, 0.0, pltpu.roll(v, 31, 1))
    return west + east + pltpu.roll(v + jnp.where(odd, before, after), 64, 2)


def mid_cross(v):
    shape = v.shape
    lane, row = iota(shape, 2), iota(shape, 1)
    along = pltpu.roll(v, 1, 2) + pltpu.roll(v, 127, 2)
    before = jnp.where(row == 0, 0.0, pltpu.roll(v, 1, 1))
    after = jnp.where(row == 31, 0.0, pltpu.roll(v, 31, 1))
    return jnp.where(lane < 32, along + before + after, 0.0)


def relax(v, cross):
    inner = v[1:-1]
    return (1.0 - OMEGA) * inner + STEP * (cross(inner) + v[2:] + v[:-2])


def grow(v, cross):
    n = v.shape[0]
    none = jnp.zeros((1, *v.shape[1:]), jnp.float32)
    both = jnp.concatenate([none, none], axis=0)
    middle = jnp.concatenate([none, (1.0 - OMEGA) * v + STEP * cross(v), none], axis=0)
    return middle + STEP * (jnp.concatenate([both, v], axis=0) + jnp.concatenate([v, both], axis=0))


def widened(v, n):
    none = jnp.zeros((n, *v.shape[1:]), jnp.float32)
    return jnp.concatenate([none, v, none], axis=0)


def packed(planes):
    return sum(pltpu.roll(p, 32 * k, 1) if k else p for k, p in enumerate(planes))


def group(v, k):
    return pltpu.roll(v, (128 - 32 * k) % 128, v.ndim - 1) if k else v


def woven(even, odd):
    n = even.shape[0]
    v = jnp.concatenate([even[:, None], odd[:, None]], axis=1).reshape(2 * n, 32, 128)
    return jnp.where(iota(v.shape, 2) < 32, v, 0.0)


def inside(v, first, planes):
    plane = iota(v.shape, 0) + first
    return jnp.where((plane >= 0) & (plane < planes), v, 0.0)


def flat_dot(v, m):
    n = v.shape[0]
    out = jnp.dot(v.reshape(n * v.shape[1], 128), m, precision=HIGHEST, preferred_element_type=jnp.float32)
    return out.reshape(n, v.shape[1], 128)


def restrict_fine(v):
    n = v.shape[0]
    pairs = v.reshape(n // 2, 2, 32, 128)
    lane, x = iota((128, 128), 0), iota((128, 128), 1)
    average = jnp.where(((lane & 63) >> 1) == x, 0.125, 0.0)
    return flat_dot(pairs[:, 0] + pairs[:, 1], average)


def prolong_fine(v):
    n = v.shape[0]
    x, lane = iota((128, 128), 0), iota((128, 128), 1)
    spread = flat_dot(v, jnp.where(((lane & 63) >> 1) == x, 1.0, 0.0))
    return jnp.broadcast_to(spread[:, None], (n, 2, 32, 128)).reshape(2 * n, 32, 128)


def own_group(shape):
    return ((iota(shape, len(shape) - 2) >> 1) & 7) == (iota(shape, len(shape) - 1) >> 4)


def restrict_mid(low, high):
    x, lane = iota((128, 128), 0), iota((128, 128), 1)
    average = jnp.where(((lane & 15) == (x >> 1)) & (x < 32), 0.125, 0.0)
    both = jnp.dot(low + high, average, precision=HIGHEST, preferred_element_type=jnp.float32)
    both = jnp.where(own_group(both.shape), both, 0.0)
    return jnp.sum(both[:16], axis=0, keepdims=True), jnp.sum(both[16:], axis=0, keepdims=True)


def in_rows(rows):
    at = iota((8, 128), 0)
    tile = jnp.zeros((8, 128), jnp.float32)
    for k, row in enumerate(rows):
        tile = jnp.where(at == k, row, tile)
    return tile


def prolong_mid(v):
    n = v.shape[0]
    rows = jnp.concatenate(
        [jnp.broadcast_to(v[:, 0:1], (n, 16, 128)), jnp.broadcast_to(v[:, 1:2], (n, 16, 128))], axis=1
    )
    rows = jnp.where(own_group(rows.shape), rows, 0.0)
    lane, x = iota((128, 128), 0), iota((128, 128), 1)
    spread = flat_dot(rows, jnp.where(((lane & 15) == (x >> 1)) & (x < 32), 1.0, 0.0))
    return jnp.broadcast_to(spread[:, None], (n, 2, 32, 128)).reshape(2 * n, 32, 128)


def coarse_solve(source):
    shape = source.shape
    lane, row = iota(shape, 2), iota(shape, 1)
    column, group = lane & 15, lane >> 4
    zero = jnp.zeros((1, *shape[1:]), jnp.float32)
    gained = GAIN2 * source
    v = gained
    for unused in range(3):
        west = jnp.where(column == 0, 0.0, pltpu.roll(v, 1, 2))
        east = jnp.where(column == 15, 0.0, pltpu.roll(v, 127, 2))
        back, on = pltpu.roll(v, 16, 2), pltpu.roll(v, 112, 2)
        before = jnp.where(group == 0, pltpu.roll(back, 1, 1), back)
        after = jnp.where(group == 7, pltpu.roll(on, 7, 1), on)
        plane = jnp.where(row < 2, west + east + before + after, 0.0)
        below = jnp.concatenate([zero, v[:-1]], axis=0)
        above = jnp.concatenate([v[1:], zero], axis=0)
        v = (1.0 - OMEGA) * v + STEP * (plane + below + above) + gained
    return v


def kernel(
    blocks, slabs,
    orb_ref, occ_ref, count_ref, ion_ref,
    pot_ref, kin_ref,
    raw, wide, stage, planar, dens, dens_in, field, rims, kin, kin_in,
    near_f, near_g, near_h, spill, spill_in, coarse, coarse_again, padded, fine,
    load_sem, send_sem, recv_sem,
):
    me, slab = lax.axis_index("cuts"), lax.axis_index("slab")
    planes = 4 * slabs

    load = pltpu.make_async_copy(orb_ref, raw, load_sem)
    load.start()

    def cut_at(r):
        return {"cuts": lax.rem(me + r, blocks)}

    def slab_at(r):
        return {"slab": lax.rem(slab + r + slabs, slabs)}

    barrier = pltpu.get_barrier_semaphore()

    @pl.loop(1, blocks)
    def _(r):
        pl.semaphore_signal(barrier, inc=1, device_id=cut_at(r), device_id_type=MESH)

    @pl.loop(1, slabs)
    def _(r):
        pl.semaphore_signal(barrier, inc=1, device_id=slab_at(r), device_id_type=MESH)

    def copy(stage, src, dst, device):
        return pltpu.make_async_remote_copy(
            src_ref=src, dst_ref=dst, send_sem=send_sem.at[stage], recv_sem=recv_sem.at[stage],
            device_id=device, device_id_type=MESH,
        )

    def columns(c):
        return pl.ds(pl.multiple_of(c * 128, 128), 128)

    coarse_again[...] = jnp.zeros_like(coarse_again)
    square = (32, 32)
    column = jnp.sum(
        jnp.where(
            iota(square, 0) == iota(square, 1),
            jnp.broadcast_to(occ_ref[...].astype(jnp.float32), square), 0.0,
        ),
        axis=1, keepdims=True,
    ) * (1.0 / OCC_DEN)
    live = iota((32, 128), 0) < jnp.broadcast_to(count_ref[...], (32, 128))
    weight = jnp.where(live, jnp.broadcast_to(column, (32, 128)), 0.0)
    wide[...] = jnp.broadcast_to(weight[:, None], (32, 4, 128))
    load.wait()

    @pl.loop(0, blocks)
    def _(c):
        p = raw[:, :, columns(c)].astype(jnp.float32)
        dens[c] = jnp.sum(wide[...] * (p * p), axis=0)

    pl.semaphore_wait(barrier, blocks + slabs - 2)

    @pl.loop(1, blocks)
    def _(r):
        copy(0, dens.at[lax.rem(me + r, blocks)], dens_in.at[r], cut_at(r)).start()

    dens_in[0] = dens[me]

    @pl.loop(0, blocks)
    def _(c):
        stage[...] = raw[:, :, columns(c)].astype(jnp.float32).reshape(128, 128)
        for z in range(4):
            planar[z, :, columns(c)] = stage[pl.ds(z, 32, stride=4), :].astype(jnp.bfloat16)

    up, down = slab_at(1), slab_at(-1)
    rim_up = copy(1, planar.at[3], rims.at[0], up)
    rim_down = copy(2, planar.at[0], rims.at[1], down)
    rim_up.start()
    rim_down.start()

    copy(0, dens_in.at[pl.ds(1, blocks - 1)], dens_in.at[pl.ds(1, blocks - 1)], cut_at(1)).wait_recv()
    field[me] = COUPLING * (jnp.sum(dens_in[...], axis=0) - ion_ref[:, columns(me)])

    @pl.loop(1, blocks)
    def _(r):
        copy(3, field.at[me], field.at[me], cut_at(r)).start()

    lane = iota((32, 128), 1)
    x = lane & 63
    odd = lane >= 64

    def tile(z, c):
        return planar[z, :, columns(c)].astype(jnp.float32)

    def folded(v):
        return (v[:8] + v[8:16]) + (v[16:24] + v[24:])

    @pl.loop(0, blocks)
    def _(c):
        left = jnp.where(c > 0, 1.0, 0.0)
        right = jnp.where(c < blocks - 1, 1.0, 0.0)
        ps = [tile(z, c) for z in range(4)]
        rows = []
        for z in range(4):
            p = ps[z]
            along = jnp.where(x == 0, 0.0, p) - jnp.where(x == 1, 0.0, pltpu.roll(p, 2, 1))
            total = pltpu.roll(folded(weight * (along * along)), 127, 1)
            back = p - left * tile(z, lax.max(c - 1, 0))
            on = right * tile(z, lax.min(c + 1, blocks - 1)) - p
            across = jnp.where(odd, back, on)
            total += pltpu.roll(folded(weight * (across * across)), 64, 1)
            if z in (1, 2):
                steep = ps[z + 1] - ps[z - 1]
                total += folded(weight * (steep * steep))
            rows.append(jnp.sum(total, axis=0, keepdims=True) * 0.125)
        kin[c] = jnp.concatenate(rows, axis=0)

    gathered = field.at[pl.ds(0, blocks - 1)]
    copy(3, gathered, gathered, cut_at(1)).wait_recv()

    for z in range(4):
        fine[z] = field[:, z, :]
    first, mid = 4 * slab, 2 * slab
    forcing = fine[...]
    left1 = inside(grow(forcing, fine_cross), first - 1, planes)
    left2 = inside(grow(left1, fine_cross), first - 2, planes)
    left3 = inside(grow(left2, fine_cross), first - 3, planes)
    source = restrict_fine(widened(left1, 1))
    below = inside(grow(source, mid_cross), mid - 2, 2 * slabs)
    coarse[slab] = in_rows([row for k in range(3) for row in restrict_mid(below[2 * k], below[2 * k + 1])])

    @pl.loop(1, slabs)
    def _(r):
        copy(6, coarse.at[slab], coarse.at[slab], slab_at(r)).start()

    near_f[3] = packed([source[k] for k in range(4)])
    again = restrict_fine(widened(left3, 1))
    near_g[2] = packed([again[0], again[1], again[4], again[5]])
    near_h[1] = packed([again[2], again[3]])
    for away in (1, -1, 2, -2, 3, -3):
        copy(7, near_f.at[3], near_f.at[3 - away], slab_at(away)).start()
    for away in (1, -1, 2, -2):
        copy(8, near_g.at[2], near_g.at[2 - away], slab_at(away)).start()
    for away in (1, -1):
        copy(9, near_h.at[1], near_h.at[1 - away], slab_at(away)).start()
    direct = GAIN0 * (left3 + widened(left2, 1) + widened(left1, 2) + widened(forcing, 3))
    spill[0] = direct[:3]
    spill[1] = direct[7:]
    direct = direct[3:7]
    spill_up = copy(4, spill.at[1], spill_in.at[0], up)
    spill_down = copy(5, spill.at[0], spill_in.at[1], down)
    spill_up.start()
    spill_down.start()

    rim_up.wait_recv()
    rim_down.wait_recv()
    has_below = jnp.where(slab > 0, 1.0, 0.0)
    has_above = jnp.where(slab < slabs - 1, 1.0, 0.0)
    row4 = iota((4, 128), 0)

    @pl.loop(0, blocks)
    def _(c):
        low = tile(1, c) - has_below * rims[0, :, columns(c)].astype(jnp.float32)
        high = has_above * rims[1, :, columns(c)].astype(jnp.float32) - tile(2, c)
        low = jnp.sum(weight * (low * low), axis=0, keepdims=True) * 0.125
        high = jnp.sum(weight * (high * high), axis=0, keepdims=True) * 0.125
        kin[c] += jnp.where(row4 == 0, low, jnp.where(row4 == 3, high, 0.0))

    @pl.loop(1, blocks)
    def _(r):
        copy(10, kin.at[lax.rem(me + r, blocks)], kin_in.at[r], cut_at(r)).start()

    kin_in[0] = kin[me]

    all_but_one = coarse.at[pl.ds(0, slabs - 1)]
    copy(6, all_but_one, all_but_one, up).wait_recv()
    parts = coarse[...]
    none = jnp.zeros((1, 8, 128), jnp.float32)
    parts = (
        pltpu.roll(parts, 6, 1)
        + jnp.concatenate([none, pltpu.roll(parts, 4, 1)[:-1]], axis=0)
        + jnp.concatenate([parts[1:], none], axis=0)
    )
    padded[pl.ds(0, 3)] = jnp.zeros((3, 8, 128), jnp.float32)
    padded[pl.ds(slabs + 3, 3)] = jnp.zeros((3, 8, 128), jnp.float32)
    padded[pl.ds(3, slabs)] = coarse_solve(jnp.where(iota(parts.shape, 1) < 2, parts, 0.0))
    lifted = prolong_mid(padded[pl.ds(slab, 7)])
    copy(7, near_f.at[pl.ds(0, 6)], near_f.at[pl.ds(0, 6)], up).wait_recv()
    near = inside(near_f[...], slab - 3, slabs)
    none = jnp.zeros((1, 32, 128), jnp.float32)
    source = woven(
        group(near, 1) + jnp.concatenate([none, group(near, 3)[:-1]], axis=0),
        group(near, 2) + jnp.concatenate([near[1:], none], axis=0),
    )
    source = inside(source, mid - 6, 2 * slabs)
    guess = GAIN1 * source[1:13] + lifted[1:13]
    error = inside(relax(guess, mid_cross) + GAIN1 * source[2:12], mid - 4, 2 * slabs)
    spread = prolong_fine(error)[1:19]
    back1 = inside(relax(spread, fine_cross), first - 6, planes)
    back2 = inside(relax(back1, fine_cross), first - 5, planes)
    back3 = relax(back2, fine_cross)
    direct += back3[4:8]
    copy(8, near_g.at[pl.ds(0, 4)], near_g.at[pl.ds(0, 4)], up).wait_recv()
    copy(9, near_h.at[pl.ds(0, 2)], near_h.at[pl.ds(0, 2)], up).wait_recv()
    near, own = inside(near_g[...], slab - 2, slabs), near_h[...]
    again = woven(
        own + group(near, 2)[0:3] + near[2:5],
        group(own, 1) + group(near, 1)[2:5] + group(near, 3)[0:3],
    )
    source = again - restrict_fine((back2[1:13] - back3) * (1.0 / GAIN0))
    source = inside(source, mid - 2, 2 * slabs)

    smoothed = relax(source[1:5], mid_cross)
    coarse_again[slab] = in_rows(restrict_mid(smoothed[0], smoothed[1]))
    for away in (4, -4, 3, -3, 2, -2, 1, -1):
        copy(11, coarse_again.at[slab], coarse_again.at[slab], slab_at(away)).start()

    spill_up.wait_recv()
    spill_down.wait_recv()
    direct += jnp.concatenate([spill_in[0], none], axis=0) + jnp.concatenate([none, spill_in[1]], axis=0)
    some = coarse_again.at[pl.ds(0, 8)]
    copy(11, some, some, up).wait_recv()
    padded[pl.ds(3, slabs)] = coarse_solve(coarse_again[...])
    lifted = prolong_mid(padded[pl.ds(slab + 2, 3)])
    guess = GAIN1 * source + lifted
    error = inside(relax(guess, mid_cross) + GAIN1 * source[1:5], mid - 1, 2 * slabs)
    fine[...] = direct + relax(prolong_fine(error)[1:7], fine_cross)
    for c in range(blocks):
        pot_ref[:, c * 128 : (c + 1) * 128] = fine[:, c, :]

    copy(10, kin_in.at[pl.ds(1, blocks - 1)], kin_in.at[pl.ds(1, blocks - 1)], cut_at(1)).wait_recv()
    kin_ref[...] = jnp.sum(kin_in[...], axis=0)

    copy(0, dens_in.at[pl.ds(1, blocks - 1)], dens_in.at[pl.ds(1, blocks - 1)], cut_at(1)).wait_send()
    rim_up.wait_send()
    rim_down.wait_send()
    copy(3, gathered, gathered, cut_at(1)).wait_send()
    spill_up.wait_send()
    spill_down.wait_send()
    copy(6, all_but_one, all_but_one, up).wait_send()
    copy(7, near_f.at[pl.ds(0, 6)], near_f.at[pl.ds(0, 6)], up).wait_send()
    copy(8, near_g.at[pl.ds(0, 4)], near_g.at[pl.ds(0, 4)], up).wait_send()
    copy(9, near_h.at[pl.ds(0, 2)], near_h.at[pl.ds(0, 2)], up).wait_send()
    copy(10, kin_in.at[pl.ds(1, blocks - 1)], kin_in.at[pl.ds(1, blocks - 1)], cut_at(1)).wait_send()
    copy(11, some, some, up).wait_send()


def solution(mesh):
    blocks, slabs = mesh.shape["cuts"], mesh.shape["slab"]

    def shards(orbitals, occupation, state_counts, ion_charge):
        f32, bf16 = jnp.float32, jnp.bfloat16
        vmem = pl.BlockSpec(memory_space=pltpu.VMEM)
        return pl.pallas_call(
            functools.partial(kernel, blocks, slabs),
            out_shape=(jax.ShapeDtypeStruct((4, 4096), f32), jax.ShapeDtypeStruct((4, 128), f32)),
            in_specs=[pl.BlockSpec(memory_space=pl.ANY), vmem, vmem, vmem],
            out_specs=(vmem, vmem),
            scratch_shapes=[
                pltpu.VMEM((32, 4, 4096), bf16),
                pltpu.VMEM((32, 4, 128), f32),
                pltpu.VMEM((128, 128), f32),
                pltpu.VMEM((4, 32, 4096), bf16),
                pltpu.VMEM((blocks, 4, 128), f32),
                pltpu.VMEM((blocks, 4, 128), f32),
                pltpu.VMEM((blocks, 4, 128), f32),
                pltpu.VMEM((2, 32, 4096), bf16),
                pltpu.VMEM((blocks, 4, 128), f32),
                pltpu.VMEM((blocks, 4, 128), f32),
                pltpu.VMEM((7, 32, 128), f32),
                pltpu.VMEM((5, 32, 128), f32),
                pltpu.VMEM((3, 32, 128), f32),
                pltpu.VMEM((2, 3, 32, 128), f32),
                pltpu.VMEM((2, 3, 32, 128), f32),
                pltpu.VMEM((slabs, 8, 128), f32),
                pltpu.VMEM((slabs, 8, 128), f32),
                pltpu.VMEM((slabs + 6, 8, 128), f32),
                pltpu.VMEM((4, 32, 128), f32),
                pltpu.SemaphoreType.DMA,
                pltpu.SemaphoreType.DMA((12,)),
                pltpu.SemaphoreType.DMA((12,)),
            ],
            compiler_params=pltpu.CompilerParams(collective_id=0, has_side_effects=True),
        )(orbitals, occupation, state_counts.reshape(1, 1), ion_charge)

    return jax.shard_map(
        shards,
        mesh=mesh,
        in_specs=(P("cuts", "slab", None), P("cuts", None), P("cuts"), P("slab", None)),
        out_specs=(P("slab", None), P("slab", "cuts")),
        check_vma=False,
    )
```

```python
import functools

import jax
import jax.numpy as jnp
from jax import lax
from jax.experimental import pallas as pl
from jax.experimental.pallas import tpu as pltpu
from jax.sharding import PartitionSpec as P

MESH = pl.DeviceIdType.MESH
HIGHEST = lax.Precision.HIGHEST
NX = 64
OCC_DEN = 8
OMEGA = 0.8
COUPLING = 4.0
STEP = OMEGA / 6.0
GAIN0, GAIN1, GAIN2 = STEP, 4.0 * STEP, 16.0 * STEP


def iota(shape, axis):
    return lax.broadcasted_iota(jnp.int32, shape, axis)


def fine_cross(v):
    shape = v.shape
    lane, row = iota(shape, 2), iota(shape, 1)
    column = lane & 63
    west = jnp.where(column == 0, 0.0, pltpu.roll(v, 1, 2))
    east = jnp.where(column == 63, 0.0, pltpu.roll(v, 127, 2))
    odd = lane >= 64
    before = jnp.where(row == 0, 0.0, pltpu.roll(v, 1, 1))
    after = jnp.where(row == 31, 0.0, pltpu.roll(v, 31, 1))
    return west + east + pltpu.roll(v + jnp.where(odd, before, after), 64, 2)


def mid_cross(v):
    shape = v.shape
    lane, row = iota(shape, 2), iota(shape, 1)
    along = pltpu.roll(v, 1, 2) + pltpu.roll(v, 127, 2)
    before = jnp.where(row == 0, 0.0, pltpu.roll(v, 1, 1))
    after = jnp.where(row == 31, 0.0, pltpu.roll(v, 31, 1))
    return jnp.where(lane < 32, along + before + after, 0.0)


def relax(v, cross):
    inner = v[1:-1]
    return (1.0 - OMEGA) * inner + STEP * (cross(inner) + v[2:] + v[:-2])


def grow(v, cross):
    n = v.shape[0]
    none = jnp.zeros((1, *v.shape[1:]), jnp.float32)
    both = jnp.concatenate([none, none], axis=0)
    middle = jnp.concatenate([none, (1.0 - OMEGA) * v + STEP * cross(v), none], axis=0)
    return middle + STEP * (jnp.concatenate([both, v], axis=0) + jnp.concatenate([v, both], axis=0))


def widened(v, n):
    none = jnp.zeros((n, *v.shape[1:]), jnp.float32)
    return jnp.concatenate([none, v, none], axis=0)


def packed(planes):
    return sum(pltpu.roll(p, 32 * k, 1) if k else p for k, p in enumerate(planes))


def group(v, k):
    return pltpu.roll(v, (128 - 32 * k) % 128, v.ndim - 1) if k else v


def woven(even, odd):
    n = even.shape[0]
    v = jnp.concatenate([even[:, None], odd[:, None]], axis=1).reshape(2 * n, 32, 128)
    return jnp.where(iota(v.shape, 2) < 32, v, 0.0)


def inside(v, first, planes):
    plane = iota(v.shape, 0) + first
    return jnp.where((plane >= 0) & (plane < planes), v, 0.0)


def flat_dot(v, m):
    n = v.shape[0]
    out = jnp.dot(v.reshape(n * v.shape[1], 128), m, precision=HIGHEST, preferred_element_type=jnp.float32)
    return out.reshape(n, v.shape[1], 128)


def restrict_fine(v):
    n = v.shape[0]
    pairs = v.reshape(n // 2, 2, 32, 128)
    lane, x = iota((128, 128), 0), iota((128, 128), 1)
    average = jnp.where(((lane & 63) >> 1) == x, 0.125, 0.0)
    return flat_dot(pairs[:, 0] + pairs[:, 1], average)


def prolong_fine(v):
    n = v.shape[0]
    x, lane = iota((128, 128), 0), iota((128, 128), 1)
    spread = flat_dot(v, jnp.where(((lane & 63) >> 1) == x, 1.0, 0.0))
    return jnp.broadcast_to(spread[:, None], (n, 2, 32, 128)).reshape(2 * n, 32, 128)


def own_group(shape):
    return ((iota(shape, len(shape) - 2) >> 1) & 7) == (iota(shape, len(shape) - 1) >> 4)


def restrict_mid(low, high):
    x, lane = iota((128, 128), 0), iota((128, 128), 1)
    average = jnp.where(((lane & 15) == (x >> 1)) & (x < 32), 0.125, 0.0)
    both = jnp.dot(low + high, average, precision=HIGHEST, preferred_element_type=jnp.float32)
    both = jnp.where(own_group(both.shape), both, 0.0)
    return jnp.sum(both[:16], axis=0, keepdims=True), jnp.sum(both[16:], axis=0, keepdims=True)


def in_rows(rows):
    at = iota((8, 128), 0)
    tile = jnp.zeros((8, 128), jnp.float32)
    for k, row in enumerate(rows):
        tile = jnp.where(at == k, row, tile)
    return tile


def prolong_mid(v):
    n = v.shape[0]
    rows = jnp.concatenate(
        [jnp.broadcast_to(v[:, 0:1], (n, 16, 128)), jnp.broadcast_to(v[:, 1:2], (n, 16, 128))], axis=1
    )
    rows = jnp.where(own_group(rows.shape), rows, 0.0)
    lane, x = iota((128, 128), 0), iota((128, 128), 1)
    spread = flat_dot(rows, jnp.where(((lane & 15) == (x >> 1)) & (x < 32), 1.0, 0.0))
    return jnp.broadcast_to(spread[:, None], (n, 2, 32, 128)).reshape(2 * n, 32, 128)


def coarse_solve(source):
    shape = source.shape
    lane, row = iota(shape, 2), iota(shape, 1)
    column, group = lane & 15, lane >> 4
    zero = jnp.zeros((1, *shape[1:]), jnp.float32)
    gained = GAIN2 * source
    v = gained
    for unused in range(3):
        west = jnp.where(column == 0, 0.0, pltpu.roll(v, 1, 2))
        east = jnp.where(column == 15, 0.0, pltpu.roll(v, 127, 2))
        back, on = pltpu.roll(v, 16, 2), pltpu.roll(v, 112, 2)
        before = jnp.where(group == 0, pltpu.roll(back, 1, 1), back)
        after = jnp.where(group == 7, pltpu.roll(on, 7, 1), on)
        plane = jnp.where(row < 2, west + east + before + after, 0.0)
        below = jnp.concatenate([zero, v[:-1]], axis=0)
        above = jnp.concatenate([v[1:], zero], axis=0)
        v = (1.0 - OMEGA) * v + STEP * (plane + below + above) + gained
    return v


def far_first(n):
    return sorted(range(n), key=lambda step: -min(step, n - step))


def kernel(
    blocks, slabs,
    orb_ref, occ_ref, count_ref, ion_ref,
    pot_ref, kin_ref,
    raw, wide, stage, planar, dens, dens_in, field, rims, kin, kin_in,
    near_f, near_g, near_h, spill, spill_in, coarse, coarse_again, padded, fine,
    load_sem, send_sem, recv_sem,
):
    me, slab = lax.axis_index("cuts"), lax.axis_index("slab")
    planes = 4 * slabs

    load = pltpu.make_async_copy(orb_ref, raw, load_sem)
    load.start()

    ring = blocks // 4
    half, y, core = me // (2 * ring), lax.rem(me // 2, ring), lax.rem(me, 2)
    others = [
        (h * ring + lax.rem(y + step, ring)) * 2 + c
        for step in far_first(ring)
        for h in (1 - half, half)
        for c in (1 - core, core)
    ][:-1]

    def cut_at(number):
        return {"cuts": number}

    def slab_at(r):
        return {"slab": lax.rem(slab + r + slabs, slabs)}

    other_slabs = [slab_at(step) for step in far_first(slabs)[:-1]]

    up, down, down_cut = slab_at(1), slab_at(-1), cut_at(others[-1])
    barrier = pltpu.get_barrier_semaphore()

    for device in [cut_at(number) for number in others] + other_slabs:
        pl.semaphore_signal(barrier, inc=1, device_id=device, device_id_type=MESH)

    def copy(stage, src, dst, device):
        return pltpu.make_async_remote_copy(
            src_ref=src, dst_ref=dst, send_sem=send_sem.at[stage], recv_sem=recv_sem.at[stage],
            device_id=device, device_id_type=MESH,
        )

    def columns(c):
        return pl.ds(pl.multiple_of(c * 128, 128), 128)

    coarse_again[...] = jnp.zeros_like(coarse_again)
    square = (32, 32)
    column = jnp.sum(
        jnp.where(
            iota(square, 0) == iota(square, 1),
            jnp.broadcast_to(occ_ref[...].astype(jnp.float32), square), 0.0,
        ),
        axis=1, keepdims=True,
    ) * (1.0 / OCC_DEN)
    live = iota((32, 128), 0) < count_ref[0]
    weight = jnp.where(live, jnp.broadcast_to(column, (32, 128)), 0.0)
    wide[...] = jnp.broadcast_to(weight[:, None], (32, 4, 128))
    load.wait()

    @pl.loop(0, blocks)
    def _(c):
        p = raw[:, :, columns(c)].astype(jnp.float32)
        dens[c] = jnp.sum(wide[...] * (p * p), axis=0)

    pl.semaphore_wait(barrier, blocks + slabs - 2)

    for k, number in enumerate(others):
        copy(0, dens.at[number], dens_in.at[k], cut_at(number)).start()

    dens_in[blocks - 1] = dens[me]

    @pl.loop(0, blocks)
    def _(c):
        stage[...] = raw[:, :, columns(c)].astype(jnp.float32).reshape(128, 128)
        for z in range(4):
            planar[z, :, columns(c)] = stage[pl.ds(z, 32, stride=4), :].astype(jnp.bfloat16)

    def rim_copies(k):
        states = pl.ds(16 * k, 16)
        return (
            copy(1 + k, planar.at[3, states], rims.at[0, states], up),
            copy(12 + k, planar.at[0, states], rims.at[1, states], down),
        )

    for rim in rim_copies(0):
        rim.start()

    lane = iota((32, 128), 1)
    x = lane & 63
    odd = lane >= 64

    def tile(z, c):
        return planar[z, :, columns(c)].astype(jnp.float32)

    def folded(v):
        return (v[:8] + v[8:16]) + (v[16:24] + v[24:])

    def plain_terms(c):
        left = jnp.where(c > 0, 1.0, 0.0)
        right = jnp.where(c < blocks - 1, 1.0, 0.0)
        ps = [tile(z, c) for z in range(4)]
        rows = []
        for z in range(4):
            p = ps[z]
            along = jnp.where(x == 0, 0.0, p) - jnp.where(x == 1, 0.0, pltpu.roll(p, 2, 1))
            total = pltpu.roll(folded(weight * (along * along)), 127, 1)
            back = p - left * tile(z, lax.max(c - 1, 0))
            on = right * tile(z, lax.min(c + 1, blocks - 1)) - p
            across = jnp.where(odd, back, on)
            total += pltpu.roll(folded(weight * (across * across)), 64, 1)
            if z in (1, 2):
                steep = ps[z + 1] - ps[z - 1]
                total += folded(weight * (steep * steep))
            rows.append(jnp.sum(total, axis=0, keepdims=True) * 0.125)
        kin[c] = jnp.concatenate(rows, axis=0)

    early = 3 * blocks // 8
    pl.loop(0, early)(plain_terms)

    copy(0, dens_in.at[pl.ds(0, blocks - 1)], dens_in.at[pl.ds(0, blocks - 1)], down_cut).wait_recv()
    field[me] = COUPLING * (jnp.sum(dens_in[...], axis=0) - ion_ref[:, columns(me)])

    for number in others:
        copy(3, field.at[me], field.at[me], cut_at(number)).start()

    for rim in rim_copies(1):
        rim.start()

    pl.loop(early, blocks)(plain_terms)

    gathered = field.at[pl.ds(0, blocks - 1)]
    copy(3, gathered, gathered, down_cut).wait_recv()

    for z in range(4):
        fine[z] = field[:, z, :]
    first, mid = 4 * slab, 2 * slab
    forcing = fine[...]
    left1 = inside(grow(forcing, fine_cross), first - 1, planes)
    source = restrict_fine(widened(left1, 1))
    below = inside(grow(source, mid_cross), mid - 2, 2 * slabs)
    coarse[slab] = in_rows([row for k in range(3) for row in restrict_mid(below[2 * k], below[2 * k + 1])])

    for device in other_slabs:
        copy(6, coarse.at[slab], coarse.at[slab], device).start()

    near_f[3] = packed([source[k] for k in range(4)])
    for away in (1, -1, 2, -2, 3, -3):
        copy(7, near_f.at[3], near_f.at[3 - away], slab_at(away)).start()
    left2 = inside(grow(left1, fine_cross), first - 2, planes)
    left3 = inside(grow(left2, fine_cross), first - 3, planes)
    again = restrict_fine(widened(left3, 1))
    near_g[2] = packed([again[0], again[1], again[4], again[5]])
    near_h[1] = packed([again[2], again[3]])
    for away in (1, -1, 2, -2):
        copy(8, near_g.at[2], near_g.at[2 - away], slab_at(away)).start()
    for away in (1, -1):
        copy(9, near_h.at[1], near_h.at[1 - away], slab_at(away)).start()
    direct = GAIN0 * (left3 + widened(left2, 1) + widened(left1, 2) + widened(forcing, 3))
    spill[0] = direct[:3]
    spill[1] = direct[7:]
    direct = direct[3:7]
    spill_up = copy(4, spill.at[1], spill_in.at[0], up)
    spill_down = copy(5, spill.at[0], spill_in.at[1], down)
    spill_up.start()
    spill_down.start()

    for k in range(2):
        for rim in rim_copies(k):
            rim.wait_recv()
    has_below = jnp.where(slab > 0, 1.0, 0.0)
    has_above = jnp.where(slab < slabs - 1, 1.0, 0.0)
    row4 = iota((4, 128), 0)

    @pl.loop(0, blocks)
    def _(c):
        low = tile(1, c) - has_below * rims[0, :, columns(c)].astype(jnp.float32)
        high = has_above * rims[1, :, columns(c)].astype(jnp.float32) - tile(2, c)
        low = jnp.sum(weight * (low * low), axis=0, keepdims=True) * 0.125
        high = jnp.sum(weight * (high * high), axis=0, keepdims=True) * 0.125
        kin[c] += jnp.where(row4 == 0, low, jnp.where(row4 == 3, high, 0.0))

    for k, number in enumerate(others):
        copy(10, kin.at[number], kin_in.at[k], cut_at(number)).start()

    kin_in[blocks - 1] = kin[me]

    all_but_one = coarse.at[pl.ds(0, slabs - 1)]
    copy(6, all_but_one, all_but_one, up).wait_recv()
    parts = coarse[...]
    none = jnp.zeros((1, 8, 128), jnp.float32)
    parts = (
        pltpu.roll(parts, 6, 1)
        + jnp.concatenate([none, pltpu.roll(parts, 4, 1)[:-1]], axis=0)
        + jnp.concatenate([parts[1:], none], axis=0)
    )
    padded[pl.ds(0, 3)] = jnp.zeros((3, 8, 128), jnp.float32)
    padded[pl.ds(slabs + 3, 3)] = jnp.zeros((3, 8, 128), jnp.float32)
    padded[pl.ds(3, slabs)] = coarse_solve(jnp.where(iota(parts.shape, 1) < 2, parts, 0.0))
    lifted = prolong_mid(padded[pl.ds(slab, 7)])
    copy(7, near_f.at[pl.ds(0, 6)], near_f.at[pl.ds(0, 6)], up).wait_recv()
    near = inside(near_f[...], slab - 3, slabs)
    none = jnp.zeros((1, 32, 128), jnp.float32)
    source = woven(
        group(near, 1) + jnp.concatenate([none, group(near, 3)[:-1]], axis=0),
        group(near, 2) + jnp.concatenate([near[1:], none], axis=0),
    )
    source = inside(source, mid - 6, 2 * slabs)
    guess = GAIN1 * source[1:13] + lifted[1:13]
    error = inside(relax(guess, mid_cross) + GAIN1 * source[2:12], mid - 4, 2 * slabs)
    spread = prolong_fine(error)[1:19]
    back1 = inside(relax(spread, fine_cross), first - 6, planes)
    back2 = inside(relax(back1, fine_cross), first - 5, planes)
    back3 = relax(back2, fine_cross)
    direct += back3[4:8]
    copy(8, near_g.at[pl.ds(0, 4)], near_g.at[pl.ds(0, 4)], up).wait_recv()
    copy(9, near_h.at[pl.ds(0, 2)], near_h.at[pl.ds(0, 2)], up).wait_recv()
    near, own = inside(near_g[...], slab - 2, slabs), near_h[...]
    again = woven(
        own + group(near, 2)[0:3] + near[2:5],
        group(own, 1) + group(near, 1)[2:5] + group(near, 3)[0:3],
    )
    source = again - restrict_fine((back2[1:13] - back3) * (1.0 / GAIN0))
    source = inside(source, mid - 2, 2 * slabs)

    smoothed = relax(source[1:5], mid_cross)
    coarse_again[slab] = in_rows(restrict_mid(smoothed[0], smoothed[1]))
    for away in (4, -4, 3, -3, 2, -2, 1, -1):
        copy(11, coarse_again.at[slab], coarse_again.at[slab], slab_at(away)).start()

    spill_up.wait_recv()
    spill_down.wait_recv()
    direct += jnp.concatenate([spill_in[0], none], axis=0) + jnp.concatenate([none, spill_in[1]], axis=0)
    some = coarse_again.at[pl.ds(0, 8)]
    copy(11, some, some, up).wait_recv()
    padded[pl.ds(3, slabs)] = coarse_solve(coarse_again[...])
    lifted = prolong_mid(padded[pl.ds(slab + 2, 3)])
    guess = GAIN1 * source + lifted
    error = inside(relax(guess, mid_cross) + GAIN1 * source[1:5], mid - 1, 2 * slabs)
    fine[...] = direct + relax(prolong_fine(error)[1:7], fine_cross)
    for c in range(blocks):
        pot_ref[:, c * 128 : (c + 1) * 128] = fine[:, c, :]

    copy(10, kin_in.at[pl.ds(0, blocks - 1)], kin_in.at[pl.ds(0, blocks - 1)], down_cut).wait_recv()
    kin_ref[...] = jnp.sum(kin_in[...], axis=0)

    copy(0, dens_in.at[pl.ds(0, blocks - 1)], dens_in.at[pl.ds(0, blocks - 1)], down_cut).wait_send()
    for k in range(2):
        for rim in rim_copies(k):
            rim.wait_send()
    copy(3, gathered, gathered, down_cut).wait_send()
    spill_up.wait_send()
    spill_down.wait_send()
    copy(6, all_but_one, all_but_one, up).wait_send()
    copy(7, near_f.at[pl.ds(0, 6)], near_f.at[pl.ds(0, 6)], up).wait_send()
    copy(8, near_g.at[pl.ds(0, 4)], near_g.at[pl.ds(0, 4)], up).wait_send()
    copy(9, near_h.at[pl.ds(0, 2)], near_h.at[pl.ds(0, 2)], up).wait_send()
    copy(10, kin_in.at[pl.ds(0, blocks - 1)], kin_in.at[pl.ds(0, blocks - 1)], down_cut).wait_send()
    copy(11, some, some, up).wait_send()


def solution(mesh):
    blocks, slabs = mesh.shape["cuts"], mesh.shape["slab"]

    def shards(orbitals, occupation, state_counts, ion_charge):
        f32, bf16 = jnp.float32, jnp.bfloat16
        vmem, smem = pl.BlockSpec(memory_space=pltpu.VMEM), pl.BlockSpec(memory_space=pltpu.SMEM)
        return pl.pallas_call(
            functools.partial(kernel, blocks, slabs),
            out_shape=(jax.ShapeDtypeStruct((4, 4096), f32), jax.ShapeDtypeStruct((4, 128), f32)),
            in_specs=[pl.BlockSpec(memory_space=pl.ANY), vmem, smem, vmem],
            out_specs=(vmem, vmem),
            scratch_shapes=[
                pltpu.VMEM((32, 4, 4096), bf16),
                pltpu.VMEM((32, 4, 128), f32),
                pltpu.VMEM((128, 128), f32),
                pltpu.VMEM((4, 32, 4096), bf16),
                pltpu.VMEM((blocks, 4, 128), f32),
                pltpu.VMEM((blocks, 4, 128), f32),
                pltpu.VMEM((blocks, 4, 128), f32),
                pltpu.VMEM((2, 32, 4096), bf16),
                pltpu.VMEM((blocks, 4, 128), f32),
                pltpu.VMEM((blocks, 4, 128), f32),
                pltpu.VMEM((7, 32, 128), f32),
                pltpu.VMEM((5, 32, 128), f32),
                pltpu.VMEM((3, 32, 128), f32),
                pltpu.VMEM((2, 3, 32, 128), f32),
                pltpu.VMEM((2, 3, 32, 128), f32),
                pltpu.VMEM((slabs, 8, 128), f32),
                pltpu.VMEM((slabs, 8, 128), f32),
                pltpu.VMEM((slabs + 6, 8, 128), f32),
                pltpu.VMEM((4, 32, 128), f32),
                pltpu.SemaphoreType.DMA,
                pltpu.SemaphoreType.DMA((14,)),
                pltpu.SemaphoreType.DMA((14,)),
            ],
            compiler_params=pltpu.CompilerParams(collective_id=0, has_side_effects=True, vmem_limit_bytes=55_930_000),
        )(orbitals, occupation, state_counts, ion_charge)

    return jax.shard_map(
        shards,
        mesh=mesh,
        in_specs=(P("cuts", "slab", None), P("cuts", None), P("cuts"), P("slab", None)),
        out_specs=(P("slab", None), P("slab", "cuts")),
        check_vma=False,
    )
```

```python
import functools

import jax
import jax.numpy as jnp
from jax import lax
from jax.experimental import pallas as pl
from jax.experimental.pallas import tpu as pltpu
from jax.sharding import PartitionSpec as P

MESH = pl.DeviceIdType.MESH
NX = 64
OCC_DEN = 8
OMEGA = 0.8
COUPLING = 4.0
STEP = OMEGA / 6.0
GAIN0, GAIN1, GAIN2 = STEP, 4.0 * STEP, 16.0 * STEP


def iota(shape, axis):
    return lax.broadcasted_iota(jnp.int32, shape, axis)


def fine_cross(v):
    shape = v.shape
    lane, row = iota(shape, 2), iota(shape, 1)
    column = lane & 63
    west = jnp.where(column == 0, 0.0, pltpu.roll(v, 1, 2))
    east = jnp.where(column == 63, 0.0, pltpu.roll(v, 127, 2))
    odd = lane >= 64
    before = jnp.where(row == 0, 0.0, pltpu.roll(v, 1, 1))
    after = jnp.where(row == 31, 0.0, pltpu.roll(v, 31, 1))
    return west + east + pltpu.roll(v + jnp.where(odd, before, after), 64, 2)


def mid_cross(v):
    shape = v.shape
    lane, row = iota(shape, 2), iota(shape, 1)
    along = pltpu.roll(v, 1, 2) + pltpu.roll(v, 127, 2)
    before = jnp.where(row == 0, 0.0, pltpu.roll(v, 1, 1))
    after = jnp.where(row == 31, 0.0, pltpu.roll(v, 31, 1))
    return jnp.where(lane < 32, along + before + after, 0.0)


def relax(v, cross):
    inner = v[1:-1]
    return (1.0 - OMEGA) * inner + STEP * (cross(inner) + v[2:] + v[:-2])


def grow(v, cross):
    n = v.shape[0]
    none = jnp.zeros((1, *v.shape[1:]), jnp.float32)
    both = jnp.concatenate([none, none], axis=0)
    middle = jnp.concatenate([none, (1.0 - OMEGA) * v + STEP * cross(v), none], axis=0)
    return middle + STEP * (jnp.concatenate([both, v], axis=0) + jnp.concatenate([v, both], axis=0))


def widened(v, n):
    none = jnp.zeros((n, *v.shape[1:]), jnp.float32)
    return jnp.concatenate([none, v, none], axis=0)


def packed(planes):
    return sum(pltpu.roll(p, 32 * k, 1) if k else p for k, p in enumerate(planes))


def group(v, k):
    return pltpu.roll(v, (128 - 32 * k) % 128, v.ndim - 1) if k else v


def woven(even, odd):
    n = even.shape[0]
    v = jnp.concatenate([even[:, None], odd[:, None]], axis=1).reshape(2 * n, 32, 128)
    return jnp.where(iota(v.shape, 2) < 32, v, 0.0)


def inside(v, first, planes):
    plane = iota(v.shape, 0) + first
    return jnp.where((plane >= 0) & (plane < planes), v, 0.0)


def exact_dot(v, m):
    m = m.astype(jnp.bfloat16)
    total = None
    for unused in range(3):
        part = v.astype(jnp.bfloat16)
        v = v - part.astype(jnp.float32)
        term = jnp.dot(part, m, preferred_element_type=jnp.float32)
        total = term if total is None else total + term
    return total


def flat_dot(v, m):
    n = v.shape[0]
    return exact_dot(v.reshape(n * v.shape[1], 128), m).reshape(n, v.shape[1], 128)


def restrict_fine(v):
    n = v.shape[0]
    pairs = v.reshape(n // 2, 2, 32, 128)
    lane, x = iota((128, 128), 0), iota((128, 128), 1)
    average = jnp.where(((lane & 63) >> 1) == x, 0.125, 0.0)
    return flat_dot(pairs[:, 0] + pairs[:, 1], average)


def prolong_fine(v):
    n = v.shape[0]
    x, lane = iota((128, 128), 0), iota((128, 128), 1)
    spread = flat_dot(v, jnp.where(((lane & 63) >> 1) == x, 1.0, 0.0))
    return jnp.broadcast_to(spread[:, None], (n, 2, 32, 128)).reshape(2 * n, 32, 128)


def own_group(shape):
    return ((iota(shape, len(shape) - 2) >> 1) & 7) == (iota(shape, len(shape) - 1) >> 4)


def restrict_mid(low, high):
    x, lane = iota((128, 128), 0), iota((128, 128), 1)
    average = jnp.where(((lane & 15) == (x >> 1)) & (x < 32), 0.125, 0.0)
    both = exact_dot(low + high, average)
    both = jnp.where(own_group(both.shape), both, 0.0)
    return jnp.sum(both[:16], axis=0, keepdims=True), jnp.sum(both[16:], axis=0, keepdims=True)


def in_rows(rows):
    at = iota((8, 128), 0)
    tile = jnp.zeros((8, 128), jnp.float32)
    for k, row in enumerate(rows):
        tile = jnp.where(at == k, row, tile)
    return tile


def prolong_mid(v):
    n = v.shape[0]
    rows = jnp.concatenate(
        [jnp.broadcast_to(v[:, 0:1], (n, 16, 128)), jnp.broadcast_to(v[:, 1:2], (n, 16, 128))], axis=1
    )
    rows = jnp.where(own_group(rows.shape), rows, 0.0)
    lane, x = iota((128, 128), 0), iota((128, 128), 1)
    spread = flat_dot(rows, jnp.where(((lane & 15) == (x >> 1)) & (x < 32), 1.0, 0.0))
    return jnp.broadcast_to(spread[:, None], (n, 2, 32, 128)).reshape(2 * n, 32, 128)


def coarse_solve(source):
    shape = source.shape
    lane, row = iota(shape, 2), iota(shape, 1)
    column, group = lane & 15, lane >> 4
    zero = jnp.zeros((1, *shape[1:]), jnp.float32)
    gained = GAIN2 * source
    v = gained
    for unused in range(3):
        west = jnp.where(column == 0, 0.0, pltpu.roll(v, 1, 2))
        east = jnp.where(column == 15, 0.0, pltpu.roll(v, 127, 2))
        back, on = pltpu.roll(v, 16, 2), pltpu.roll(v, 112, 2)
        before = jnp.where(group == 0, pltpu.roll(back, 1, 1), back)
        after = jnp.where(group == 7, pltpu.roll(on, 7, 1), on)
        plane = jnp.where(row < 2, west + east + before + after, 0.0)
        below = jnp.concatenate([zero, v[:-1]], axis=0)
        above = jnp.concatenate([v[1:], zero], axis=0)
        v = (1.0 - OMEGA) * v + STEP * (plane + below + above) + gained
    return v


def far_first(n):
    return sorted(range(n), key=lambda step: -min(step, n - step))


def kernel(
    blocks, slabs,
    orb_ref, occ_ref, count_ref, ion_ref,
    pot_ref, kin_ref,
    occ, ion, raw, wide, stage, planar, dens, dens_in, field, rims, kin, kin_in,
    near, low_near, own_near, spill, spill_in, coarse, coarse_again, padded, fine,
    load_sem, send_sem, recv_sem,
):
    me, slab = lax.axis_index("cuts"), lax.axis_index("slab")
    planes = 4 * slabs

    load = pltpu.make_async_copy(orb_ref, raw, load_sem.at[0])
    load_small = pltpu.make_async_copy(occ_ref, occ, load_sem.at[1])
    load_ion = pltpu.make_async_copy(ion_ref, ion, load_sem.at[2])
    load_small.start()
    load.start()
    load_ion.start()

    ring = blocks // 4
    half, y, core = me // (2 * ring), lax.rem(me // 2, ring), lax.rem(me, 2)
    others = [
        (h * ring + lax.rem(y + step, ring)) * 2 + c
        for step in far_first(ring)
        for h in (1 - half, half)
        for c in (1 - core, core)
    ][:-1]

    def cut_at(number):
        return {"cuts": number}

    def slab_at(r):
        return {"slab": lax.rem(slab + r + slabs, slabs)}

    other_slabs = [slab_at(step) for step in far_first(slabs)[:-1]]

    up, down, down_cut = slab_at(1), slab_at(-1), cut_at(others[-1])
    barrier = pltpu.get_barrier_semaphore()

    for device in [cut_at(number) for number in others] + other_slabs:
        pl.semaphore_signal(barrier, inc=1, device_id=device, device_id_type=MESH)

    def copy(stage, src, dst, device):
        return pltpu.make_async_remote_copy(
            src_ref=src, dst_ref=dst, send_sem=send_sem.at[stage], recv_sem=recv_sem.at[stage],
            device_id=device, device_id_type=MESH,
        )

    def columns(c):
        return pl.ds(pl.multiple_of(c * 128, 128), 128)

    coarse_again[...] = jnp.zeros_like(coarse_again)
    load_small.wait()
    square = (32, 32)
    column = jnp.sum(
        jnp.where(
            iota(square, 0) == iota(square, 1),
            jnp.broadcast_to(occ[...].astype(jnp.float32), square), 0.0,
        ),
        axis=1, keepdims=True,
    ) * (1.0 / OCC_DEN)
    live = iota((32, 128), 0) < count_ref[0]
    weight = jnp.where(live, jnp.broadcast_to(column, (32, 128)), 0.0)
    wide[...] = jnp.broadcast_to(weight[:, None], (32, 4, 128))
    load.wait()

    @pl.loop(0, blocks)
    def _(c):
        p = raw[:, :, columns(c)].astype(jnp.float32)
        dens[c] = jnp.sum(wide[...] * (p * p), axis=0)

    pl.semaphore_wait(barrier, blocks + slabs - 2)

    for k, number in enumerate(others):
        copy(0, dens.at[number], dens_in.at[k], cut_at(number)).start()

    dens_in[blocks - 1] = dens[me]

    @pl.loop(0, blocks)
    def _(c):
        stage[...] = raw[:, :, columns(c)].astype(jnp.float32).reshape(128, 128)
        for z in range(4):
            planar[z, :, columns(c)] = stage[pl.ds(z, 32, stride=4), :].astype(jnp.bfloat16)

    def rim_copies(k):
        part = pl.ds(2048 * k, 2048)
        return (
            copy(1 + k, planar.at[3, :, part], rims.at[0, :, part], up),
            copy(12 + k, planar.at[0, :, part], rims.at[1, :, part], down),
        )

    for rim in rim_copies(0):
        rim.start()

    lane = iota((32, 128), 1)
    x = lane & 63
    odd = lane >= 64

    def tile(z, c):
        return planar[z, :, columns(c)].astype(jnp.float32)

    def folded(v):
        return (v[:8] + v[8:16]) + (v[16:24] + v[24:])

    def plain_terms(c):
        left = jnp.where(c > 0, 1.0, 0.0)
        right = jnp.where(c < blocks - 1, 1.0, 0.0)
        ps = [tile(z, c) for z in range(4)]
        rows = []
        for z in range(4):
            p = ps[z]
            along = jnp.where(x == 0, 0.0, p) - jnp.where(x == 1, 0.0, pltpu.roll(p, 2, 1))
            total = pltpu.roll(folded(weight * (along * along)), 127, 1)
            back = p - left * tile(z, lax.max(c - 1, 0))
            on = right * tile(z, lax.min(c + 1, blocks - 1)) - p
            across = jnp.where(odd, back, on)
            total += pltpu.roll(folded(weight * (across * across)), 64, 1)
            if z in (1, 2):
                steep = ps[z + 1] - ps[z - 1]
                total += folded(weight * (steep * steep))
            rows.append(jnp.sum(total, axis=0, keepdims=True) * 0.125)
        kin[c] = jnp.concatenate(rows, axis=0)

    early = 3 * blocks // 8
    pl.loop(0, early)(plain_terms)

    copy(0, dens_in.at[pl.ds(0, blocks - 1)], dens_in.at[pl.ds(0, blocks - 1)], down_cut).wait_recv()
    load_ion.wait()
    field[me] = COUPLING * (jnp.sum(dens_in[...], axis=0) - ion[:, columns(me)])

    for number in others:
        copy(3, field.at[me], field.at[me], cut_at(number)).start()

    for rim in rim_copies(1):
        rim.start()

    pl.loop(early, blocks)(plain_terms)

    gathered = field.at[pl.ds(0, blocks - 1)]
    copy(3, gathered, gathered, down_cut).wait_recv()

    for z in range(4):
        fine[z] = field[:, z, :]
    first, mid = 4 * slab, 2 * slab
    forcing = fine[...]
    left1 = inside(grow(forcing, fine_cross), first - 1, planes)
    source = restrict_fine(widened(left1, 1))
    near[6] = packed([source[k] for k in range(4)])
    for k, away in enumerate((3, -3, 2, -2, 1, -1)):
        copy(7, near.at[6], near.at[k], slab_at(away)).start()
    below = inside(grow(source, mid_cross), mid - 2, 2 * slabs)
    coarse[slab] = in_rows([row for k in range(3) for row in restrict_mid(below[2 * k], below[2 * k + 1])])

    for device in other_slabs:
        copy(6, coarse.at[slab], coarse.at[slab], device).start()

    left2 = inside(grow(left1, fine_cross), first - 2, planes)
    left3 = inside(grow(left2, fine_cross), first - 3, planes)
    again = restrict_fine(widened(left3, 1))
    own_near[0] = packed([again[0], again[1], again[4], again[5]])
    own_near[1] = packed([again[2], again[3]])
    toward = 1 - 2 * core
    for k, (block, steps) in enumerate(((0, 1), (0, 2), (1, 1))):
        copy(8, own_near.at[block], low_near.at[core, k], slab_at(steps * toward)).start()
    direct = GAIN0 * (left3 + widened(left2, 1) + widened(left1, 2) + widened(forcing, 3))
    spill[0] = direct[:3]
    spill[1] = direct[7:]
    direct = direct[3:7]
    spill_over = copy(4, spill.at[1 - core], spill_in.at[core], slab_at(toward))
    spill_over.start()
    spill_pass = copy(5, spill_in.at[core], spill_in.at[core], down_cut)

    for k in range(2):
        for rim in rim_copies(k):
            rim.wait_recv()
    has_below = jnp.where(slab > 0, 1.0, 0.0)
    has_above = jnp.where(slab < slabs - 1, 1.0, 0.0)
    row4 = iota((4, 128), 0)

    @pl.loop(0, blocks)
    def _(c):
        low = tile(1, c) - has_below * rims[0, :, columns(c)].astype(jnp.float32)
        high = has_above * rims[1, :, columns(c)].astype(jnp.float32) - tile(2, c)
        low = jnp.sum(weight * (low * low), axis=0, keepdims=True) * 0.125
        high = jnp.sum(weight * (high * high), axis=0, keepdims=True) * 0.125
        kin[c] += jnp.where(row4 == 0, low, jnp.where(row4 == 3, high, 0.0))

    for k, number in enumerate(others):
        copy(10, kin.at[number], kin_in.at[k], cut_at(number)).start()

    kin_in[blocks - 1] = kin[me]

    all_but_one = coarse.at[pl.ds(0, slabs - 1)]
    copy(6, all_but_one, all_but_one, up).wait_recv()
    parts = coarse[...]
    none = jnp.zeros((1, 8, 128), jnp.float32)
    parts = (
        pltpu.roll(parts, 6, 1)
        + jnp.concatenate([none, pltpu.roll(parts, 4, 1)[:-1]], axis=0)
        + jnp.concatenate([parts[1:], none], axis=0)
    )
    padded[pl.ds(0, 3)] = jnp.zeros((3, 8, 128), jnp.float32)
    padded[pl.ds(slabs + 3, 3)] = jnp.zeros((3, 8, 128), jnp.float32)
    padded[pl.ds(3, slabs)] = coarse_solve(jnp.where(iota(parts.shape, 1) < 2, parts, 0.0))
    lifted = prolong_mid(padded[pl.ds(slab, 7)])
    copy(7, near.at[pl.ds(0, 6)], near.at[pl.ds(0, 6)], up).wait_recv()
    arrived = low_near.at[core]
    copy(8, arrived, arrived, down_cut).wait_recv()
    near_pass = copy(9, arrived, arrived, down_cut)
    near_pass.start()
    near_f = jnp.stack([near[0], near[2], near[4], near[6], near[5], near[3], near[1]])
    near_f = inside(near_f, slab - 3, slabs)
    none = jnp.zeros((1, 32, 128), jnp.float32)
    source = woven(
        group(near_f, 1) + jnp.concatenate([none, group(near_f, 3)[:-1]], axis=0),
        group(near_f, 2) + jnp.concatenate([near_f[1:], none], axis=0),
    )
    source = inside(source, mid - 6, 2 * slabs)
    guess = GAIN1 * source[1:13] + lifted[1:13]
    error = inside(relax(guess, mid_cross) + GAIN1 * source[2:12], mid - 4, 2 * slabs)
    spread = prolong_fine(error)[1:19]
    back1 = inside(relax(spread, fine_cross), first - 6, planes)
    back2 = inside(relax(back1, fine_cross), first - 5, planes)
    back3 = relax(back2, fine_cross)
    direct += back3[4:8]
    near_pass.wait_recv()
    near_g = jnp.stack([low_near[0, 1], low_near[0, 0], own_near[0], low_near[1, 0], low_near[1, 1]])
    near_g = inside(near_g, slab - 2, slabs)
    near_h = jnp.stack([low_near[0, 2], own_near[1], low_near[1, 2]])
    again = woven(
        near_h + group(near_g, 2)[0:3] + near_g[2:5],
        group(near_h, 1) + group(near_g, 1)[2:5] + group(near_g, 3)[0:3],
    )
    source = again - restrict_fine((back2[1:13] - back3) * (1.0 / GAIN0))
    source = inside(source, mid - 2, 2 * slabs)

    smoothed = relax(source[1:5], mid_cross)
    coarse_again[slab] = in_rows(restrict_mid(smoothed[0], smoothed[1]))
    for away in (4, -4, 3, -3, 2, -2, 1, -1):
        copy(11, coarse_again.at[slab], coarse_again.at[slab], slab_at(away)).start()

    spill_over.wait_recv()
    spill_pass.start()
    some = coarse_again.at[pl.ds(0, 8)]
    copy(11, some, some, up).wait_recv()
    spill_pass.wait_recv()
    direct += jnp.concatenate([spill_in[0], none], axis=0) + jnp.concatenate([none, spill_in[1]], axis=0)
    padded[pl.ds(3, slabs)] = coarse_solve(coarse_again[...])
    lifted = prolong_mid(padded[pl.ds(slab + 2, 3)])
    guess = GAIN1 * source + lifted
    error = inside(relax(guess, mid_cross) + GAIN1 * source[1:5], mid - 1, 2 * slabs)
    fine[...] = direct + relax(prolong_fine(error)[1:7], fine_cross)
    for c in range(blocks):
        pot_ref[:, c * 128 : (c + 1) * 128] = fine[:, c, :]

    copy(10, kin_in.at[pl.ds(0, blocks - 1)], kin_in.at[pl.ds(0, blocks - 1)], down_cut).wait_recv()
    kin_ref[...] = jnp.sum(kin_in[...], axis=0)

    copy(0, dens_in.at[pl.ds(0, blocks - 1)], dens_in.at[pl.ds(0, blocks - 1)], down_cut).wait_send()
    for k in range(2):
        for rim in rim_copies(k):
            rim.wait_send()
    copy(3, gathered, gathered, down_cut).wait_send()
    spill_over.wait_send()
    spill_pass.wait_send()
    copy(6, all_but_one, all_but_one, up).wait_send()
    copy(7, near.at[pl.ds(0, 6)], near.at[pl.ds(0, 6)], up).wait_send()
    copy(8, arrived, arrived, down_cut).wait_send()
    near_pass.wait_send()
    copy(10, kin_in.at[pl.ds(0, blocks - 1)], kin_in.at[pl.ds(0, blocks - 1)], down_cut).wait_send()
    copy(11, some, some, up).wait_send()


def solution(mesh):
    blocks, slabs = mesh.shape["cuts"], mesh.shape["slab"]

    def shards(orbitals, occupation, state_counts, ion_charge):
        f32, bf16 = jnp.float32, jnp.bfloat16
        anywhere, vmem = pl.BlockSpec(memory_space=pl.ANY), pl.BlockSpec(memory_space=pltpu.VMEM)
        return pl.pallas_call(
            functools.partial(kernel, blocks, slabs),
            out_shape=(jax.ShapeDtypeStruct((4, 4096), f32), jax.ShapeDtypeStruct((4, 128), f32)),
            in_specs=[anywhere, anywhere, pl.BlockSpec(memory_space=pltpu.SMEM), anywhere],
            out_specs=(vmem, vmem),
            scratch_shapes=[
                pltpu.VMEM((1, 32), jnp.int32),
                pltpu.VMEM((4, 4096), f32),
                pltpu.VMEM((32, 4, 4096), bf16),
                pltpu.VMEM((32, 4, 128), f32),
                pltpu.VMEM((128, 128), f32),
                pltpu.VMEM((4, 32, 4096), bf16),
                pltpu.VMEM((blocks, 4, 128), f32),
                pltpu.VMEM((blocks, 4, 128), f32),
                pltpu.VMEM((blocks, 4, 128), f32),
                pltpu.VMEM((2, 32, 4096), bf16),
                pltpu.VMEM((blocks, 4, 128), f32),
                pltpu.VMEM((blocks, 4, 128), f32),
                pltpu.VMEM((7, 32, 128), f32),
                pltpu.VMEM((2, 3, 32, 128), f32),
                pltpu.VMEM((2, 32, 128), f32),
                pltpu.VMEM((2, 3, 32, 128), f32),
                pltpu.VMEM((2, 3, 32, 128), f32),
                pltpu.VMEM((slabs, 8, 128), f32),
                pltpu.VMEM((slabs, 8, 128), f32),
                pltpu.VMEM((slabs + 6, 8, 128), f32),
                pltpu.VMEM((4, 32, 128), f32),
                pltpu.SemaphoreType.DMA((3,)),
                pltpu.SemaphoreType.DMA((14,)),
                pltpu.SemaphoreType.DMA((14,)),
            ],
            compiler_params=pltpu.CompilerParams(collective_id=0, has_side_effects=True, vmem_limit_bytes=55_900_000),
        )(orbitals, occupation, state_counts, ion_charge)

    return jax.shard_map(
        shards,
        mesh=mesh,
        in_specs=(P("cuts", "slab", None), P("cuts", None), P("cuts"), P("slab", None)),
        out_specs=(P("slab", None), P("slab", "cuts")),
        check_vma=False,
    )
```

```python
import functools

import jax
import jax.numpy as jnp
from jax import lax
from jax.experimental import pallas as pl
from jax.experimental.pallas import tpu as pltpu
from jax.sharding import PartitionSpec as P

MESH = pl.DeviceIdType.MESH
NX = 64
OCC_DEN = 8
OMEGA = 0.8
COUPLING = 4.0
STEP = OMEGA / 6.0
GAIN0, GAIN1, GAIN2 = STEP, 4.0 * STEP, 16.0 * STEP


def iota(shape, axis):
    return lax.broadcasted_iota(jnp.int32, shape, axis)


def fine_cross(v):
    shape = v.shape
    lane, row = iota(shape, 2), iota(shape, 1)
    column = lane & 63
    west = jnp.where(column == 0, 0.0, pltpu.roll(v, 1, 2))
    east = jnp.where(column == 63, 0.0, pltpu.roll(v, 127, 2))
    odd = lane >= 64
    before = jnp.where(row == 0, 0.0, pltpu.roll(v, 1, 1))
    after = jnp.where(row == 31, 0.0, pltpu.roll(v, 31, 1))
    return west + east + pltpu.roll(v + jnp.where(odd, before, after), 64, 2)


def mid_cross(v):
    shape = v.shape
    lane, row = iota(shape, 2), iota(shape, 1)
    along = pltpu.roll(v, 1, 2) + pltpu.roll(v, 127, 2)
    before = jnp.where(row == 0, 0.0, pltpu.roll(v, 1, 1))
    after = jnp.where(row == 31, 0.0, pltpu.roll(v, 31, 1))
    return jnp.where(lane < 32, along + before + after, 0.0)


def relax(v, cross):
    inner = v[1:-1]
    return (1.0 - OMEGA) * inner + STEP * (cross(inner) + v[2:] + v[:-2])


def grow(v, cross):
    n = v.shape[0]
    none = jnp.zeros((1, *v.shape[1:]), jnp.float32)
    both = jnp.concatenate([none, none], axis=0)
    middle = jnp.concatenate([none, (1.0 - OMEGA) * v + STEP * cross(v), none], axis=0)
    return middle + STEP * (jnp.concatenate([both, v], axis=0) + jnp.concatenate([v, both], axis=0))


def widened(v, n):
    none = jnp.zeros((n, *v.shape[1:]), jnp.float32)
    return jnp.concatenate([none, v, none], axis=0)


def packed(planes):
    return sum(pltpu.roll(p, 32 * k, 1) if k else p for k, p in enumerate(planes))


def group(v, k):
    return pltpu.roll(v, (128 - 32 * k) % 128, v.ndim - 1) if k else v


def woven(even, odd):
    n = even.shape[0]
    v = jnp.concatenate([even[:, None], odd[:, None]], axis=1).reshape(2 * n, 32, 128)
    return jnp.where(iota(v.shape, 2) < 32, v, 0.0)


def inside(v, first, planes):
    plane = iota(v.shape, 0) + first
    return jnp.where((plane >= 0) & (plane < planes), v, 0.0)


def exact_dot(v, m):
    m = m.astype(jnp.bfloat16)
    total = None
    for unused in range(3):
        part = v.astype(jnp.bfloat16)
        v = v - part.astype(jnp.float32)
        term = jnp.dot(part, m, preferred_element_type=jnp.float32)
        total = term if total is None else total + term
    return total


def flat_dot(v, m):
    n = v.shape[0]
    return exact_dot(v.reshape(n * v.shape[1], 128), m).reshape(n, v.shape[1], 128)


def restrict_fine(v):
    n = v.shape[0]
    pairs = v.reshape(n // 2, 2, 32, 128)
    lane, x = iota((128, 128), 0), iota((128, 128), 1)
    average = jnp.where(((lane & 63) >> 1) == x, 0.125, 0.0)
    return flat_dot(pairs[:, 0] + pairs[:, 1], average)


def prolong_fine(v):
    n = v.shape[0]
    x, lane = iota((128, 128), 0), iota((128, 128), 1)
    spread = flat_dot(v, jnp.where(((lane & 63) >> 1) == x, 1.0, 0.0))
    return jnp.broadcast_to(spread[:, None], (n, 2, 32, 128)).reshape(2 * n, 32, 128)


def own_group(shape):
    return ((iota(shape, len(shape) - 2) >> 1) & 7) == (iota(shape, len(shape) - 1) >> 4)


def restrict_mid(low, high):
    x, lane = iota((128, 128), 0), iota((128, 128), 1)
    average = jnp.where(((lane & 15) == (x >> 1)) & (x < 32), 0.125, 0.0)
    both = exact_dot(low + high, average)
    both = jnp.where(own_group(both.shape), both, 0.0)
    return jnp.sum(both[:16], axis=0, keepdims=True), jnp.sum(both[16:], axis=0, keepdims=True)


def in_rows(rows):
    at = iota((8, 128), 0)
    tile = jnp.zeros((8, 128), jnp.float32)
    for k, row in enumerate(rows):
        tile = jnp.where(at == k, row, tile)
    return tile


def prolong_mid(v):
    n = v.shape[0]
    rows = jnp.concatenate(
        [jnp.broadcast_to(v[:, 0:1], (n, 16, 128)), jnp.broadcast_to(v[:, 1:2], (n, 16, 128))], axis=1
    )
    rows = jnp.where(own_group(rows.shape), rows, 0.0)
    lane, x = iota((128, 128), 0), iota((128, 128), 1)
    spread = flat_dot(rows, jnp.where(((lane & 15) == (x >> 1)) & (x < 32), 1.0, 0.0))
    return jnp.broadcast_to(spread[:, None], (n, 2, 32, 128)).reshape(2 * n, 32, 128)


def coarse_solve(source):
    shape = source.shape
    lane, row = iota(shape, 2), iota(shape, 1)
    column, group = lane & 15, lane >> 4
    zero = jnp.zeros((1, *shape[1:]), jnp.float32)
    gained = GAIN2 * source
    v = gained
    for unused in range(3):
        west = jnp.where(column == 0, 0.0, pltpu.roll(v, 1, 2))
        east = jnp.where(column == 15, 0.0, pltpu.roll(v, 127, 2))
        back, on = pltpu.roll(v, 16, 2), pltpu.roll(v, 112, 2)
        before = jnp.where(group == 0, pltpu.roll(back, 1, 1), back)
        after = jnp.where(group == 7, pltpu.roll(on, 7, 1), on)
        plane = jnp.where(row < 2, west + east + before + after, 0.0)
        below = jnp.concatenate([zero, v[:-1]], axis=0)
        above = jnp.concatenate([v[1:], zero], axis=0)
        v = (1.0 - OMEGA) * v + STEP * (plane + below + above) + gained
    return v


def far_first(n):
    return sorted(range(n), key=lambda step: -min(step, n - step))


def kernel(
    blocks, slabs,
    orb_ref, occ_ref, count_ref, ion_ref,
    pot_ref, kin_ref,
    occ, ion, raw, wide, stage, planar, dens, dens_in, field, rims, kin, kin_in,
    near, low_near, own_near, spill, spill_in, coarse, coarse_again, padded, fine,
    load_sem, send_sem, recv_sem,
):
    me, slab = lax.axis_index("cuts"), lax.axis_index("slab")
    planes = 4 * slabs

    load = pltpu.make_async_copy(orb_ref, raw, load_sem.at[0])
    load_small = pltpu.make_async_copy(occ_ref, occ, load_sem.at[1])
    load_ion = pltpu.make_async_copy(ion_ref, ion, load_sem.at[2])
    load_small.start()
    load.start()
    load_ion.start()

    ring = blocks // 4
    half, y, core = me // (2 * ring), lax.rem(me // 2, ring), lax.rem(me, 2)
    others = [
        (h * ring + lax.rem(y + step, ring)) * 2 + c
        for step in far_first(ring)
        for h in (1 - half, half)
        for c in (1 - core, core)
    ][:-1]

    def cut_at(number):
        return {"cuts": number}

    def slab_at(r):
        return {"slab": lax.rem(slab + r + slabs, slabs)}

    other_slabs = [slab_at(step) for step in far_first(slabs)[:-1]]

    up, down, down_cut = slab_at(1), slab_at(-1), cut_at(others[-1])
    barrier = pltpu.get_barrier_semaphore()

    for device in [cut_at(number) for number in others] + other_slabs:
        pl.semaphore_signal(barrier, inc=1, device_id=device, device_id_type=MESH)

    def copy(stage, src, dst, device):
        return pltpu.make_async_remote_copy(
            src_ref=src, dst_ref=dst, send_sem=send_sem.at[stage], recv_sem=recv_sem.at[stage],
            device_id=device, device_id_type=MESH,
        )

    def columns(c):
        return pl.ds(pl.multiple_of(c * 128, 128), 128)

    coarse_again[...] = jnp.zeros_like(coarse_again)
    load_small.wait()
    square = (32, 32)
    column = jnp.sum(
        jnp.where(
            iota(square, 0) == iota(square, 1),
            jnp.broadcast_to(occ[...].astype(jnp.float32), square), 0.0,
        ),
        axis=1, keepdims=True,
    ) * (1.0 / OCC_DEN)
    live = iota((32, 128), 0) < count_ref[0]
    weight = jnp.where(live, jnp.broadcast_to(column, (32, 128)), 0.0)
    wide[...] = jnp.broadcast_to(weight[:, None], (32, 4, 128))
    load.wait()

    @pl.loop(0, blocks)
    def _(c):
        p = raw[:, :, columns(c)].astype(jnp.float32)
        dens[c] = jnp.sum(wide[...] * (p * p), axis=0)

    pl.semaphore_wait(barrier, blocks + slabs - 2)

    for k, number in enumerate(others):
        copy(0, dens.at[number], dens_in.at[k], cut_at(number)).start()

    dens_in[blocks - 1] = dens[me]

    @pl.loop(0, blocks)
    def _(c):
        stage[...] = raw[:, :, columns(c)].astype(jnp.float32).reshape(128, 128)
        for z in range(4):
            planar[z, :, columns(c)] = stage[pl.ds(z, 32, stride=4), :].astype(jnp.bfloat16)

    def rim_copies(k):
        part = pl.ds(2048 * k, 2048)
        return (
            copy(1 + k, planar.at[3, :, part], rims.at[0, :, part], up),
            copy(12 + k, planar.at[0, :, part], rims.at[1, :, part], down),
        )

    for rim in rim_copies(0):
        rim.start()

    lane = iota((32, 128), 1)
    x = lane & 63
    odd = lane >= 64

    def tile(z, c):
        return planar[z, :, columns(c)].astype(jnp.float32)

    def folded(v):
        return (v[:8] + v[8:16]) + (v[16:24] + v[24:])

    def plain_terms(c):
        left = jnp.where(c > 0, 1.0, 0.0)
        right = jnp.where(c < blocks - 1, 1.0, 0.0)
        ps = [tile(z, c) for z in range(4)]
        rows = []
        for z in range(4):
            p = ps[z]
            along = jnp.where(x == 0, 0.0, p) - jnp.where(x == 1, 0.0, pltpu.roll(p, 2, 1))
            total = pltpu.roll(folded(weight * (along * along)), 127, 1)
            back = p - left * tile(z, lax.max(c - 1, 0))
            on = right * tile(z, lax.min(c + 1, blocks - 1)) - p
            across = jnp.where(odd, back, on)
            total += pltpu.roll(folded(weight * (across * across)), 64, 1)
            if z in (1, 2):
                steep = ps[z + 1] - ps[z - 1]
                total += folded(weight * (steep * steep))
            rows.append(jnp.sum(total, axis=0, keepdims=True) * 0.125)
        kin[c] = jnp.concatenate(rows, axis=0)

    early = 3 * blocks // 8
    pl.loop(0, early)(plain_terms)

    copy(0, dens_in.at[pl.ds(0, blocks - 1)], dens_in.at[pl.ds(0, blocks - 1)], down_cut).wait_recv()
    load_ion.wait()
    field[me] = COUPLING * (jnp.sum(dens_in[...], axis=0) - ion[:, columns(me)])

    for number in others:
        copy(3, field.at[me], field.at[me], cut_at(number)).start()

    for rim in rim_copies(1):
        rim.start()

    pl.loop(early, blocks)(plain_terms)

    gathered = field.at[pl.ds(0, blocks - 1)]
    copy(3, gathered, gathered, down_cut).wait_recv()

    for z in range(4):
        fine[z] = field[:, z, :]
    first, mid = 4 * slab, 2 * slab
    forcing = fine[...]
    left1 = inside(grow(forcing, fine_cross), first - 1, planes)
    source = restrict_fine(widened(left1, 1))
    near[6] = packed([source[k] for k in range(4)])
    for k, away in enumerate((3, -3, 2, -2, 1, -1)):
        copy(7, near.at[6], near.at[k], slab_at(away)).start()
    below = inside(grow(source, mid_cross), mid - 2, 2 * slabs)
    coarse[slab] = in_rows([row for k in range(3) for row in restrict_mid(below[2 * k], below[2 * k + 1])])

    for device in other_slabs:
        copy(6, coarse.at[slab], coarse.at[slab], device).start()

    left2 = inside(grow(left1, fine_cross), first - 2, planes)
    left3 = inside(grow(left2, fine_cross), first - 3, planes)
    again = restrict_fine(widened(left3, 1))
    own_near[0] = packed([again[0], again[1], again[4], again[5]])
    own_near[1] = packed([again[2], again[3]])
    toward = 1 - 2 * core
    for k, (block, steps) in enumerate(((0, 1), (0, 2), (1, 1))):
        copy(8, own_near.at[block], low_near.at[core, k], slab_at(steps * toward)).start()
    direct = GAIN0 * (left3 + widened(left2, 1) + widened(left1, 2) + widened(forcing, 3))
    spill[0] = direct[:3]
    spill[1] = direct[7:]
    direct = direct[3:7]
    spill_over = copy(4, spill.at[1 - core], spill_in.at[core], slab_at(toward))
    spill_over.start()
    spill_pass = copy(5, spill_in.at[core], spill_in.at[core], down_cut)

    for k in range(2):
        for rim in rim_copies(k):
            rim.wait_recv()
    has_below = jnp.where(slab > 0, 1.0, 0.0)
    has_above = jnp.where(slab < slabs - 1, 1.0, 0.0)
    row4 = iota((4, 128), 0)

    @pl.loop(0, blocks)
    def _(c):
        low = tile(1, c) - has_below * rims[0, :, columns(c)].astype(jnp.float32)
        high = has_above * rims[1, :, columns(c)].astype(jnp.float32) - tile(2, c)
        low = jnp.sum(weight * (low * low), axis=0, keepdims=True) * 0.125
        high = jnp.sum(weight * (high * high), axis=0, keepdims=True) * 0.125
        kin[c] += jnp.where(row4 == 0, low, jnp.where(row4 == 3, high, 0.0))

    for k, number in enumerate(others):
        copy(10, kin.at[number], kin_in.at[k], cut_at(number)).start()

    kin_in[blocks - 1] = kin[me]

    all_but_one = coarse.at[pl.ds(0, slabs - 1)]
    copy(6, all_but_one, all_but_one, up).wait_recv()
    arrived = low_near.at[core]
    copy(8, arrived, arrived, down_cut).wait_recv()
    near_pass = copy(9, arrived, arrived, down_cut)
    near_pass.start()
    parts = coarse[...]
    none = jnp.zeros((1, 8, 128), jnp.float32)
    parts = (
        pltpu.roll(parts, 6, 1)
        + jnp.concatenate([none, pltpu.roll(parts, 4, 1)[:-1]], axis=0)
        + jnp.concatenate([parts[1:], none], axis=0)
    )
    padded[pl.ds(0, 3)] = jnp.zeros((3, 8, 128), jnp.float32)
    padded[pl.ds(slabs + 3, 3)] = jnp.zeros((3, 8, 128), jnp.float32)
    padded[pl.ds(3, slabs)] = coarse_solve(jnp.where(iota(parts.shape, 1) < 2, parts, 0.0))
    lifted = prolong_mid(padded[pl.ds(slab, 7)])
    copy(7, near.at[pl.ds(0, 6)], near.at[pl.ds(0, 6)], up).wait_recv()
    near_f = jnp.stack([near[0], near[2], near[4], near[6], near[5], near[3], near[1]])
    near_f = inside(near_f, slab - 3, slabs)
    none = jnp.zeros((1, 32, 128), jnp.float32)
    source = woven(
        group(near_f, 1) + jnp.concatenate([none, group(near_f, 3)[:-1]], axis=0),
        group(near_f, 2) + jnp.concatenate([near_f[1:], none], axis=0),
    )
    source = inside(source, mid - 6, 2 * slabs)
    guess = GAIN1 * source[1:13] + lifted[1:13]
    error = inside(relax(guess, mid_cross) + GAIN1 * source[2:12], mid - 4, 2 * slabs)
    spread = prolong_fine(error)[1:19]
    back1 = inside(relax(spread, fine_cross), first - 6, planes)
    back2 = inside(relax(back1, fine_cross), first - 5, planes)
    back3 = relax(back2, fine_cross)
    direct += back3[4:8]
    near_pass.wait_recv()
    near_g = jnp.stack([low_near[0, 1], low_near[0, 0], own_near[0], low_near[1, 0], low_near[1, 1]])
    near_g = inside(near_g, slab - 2, slabs)
    near_h = jnp.stack([low_near[0, 2], own_near[1], low_near[1, 2]])
    again = woven(
        near_h + group(near_g, 2)[0:3] + near_g[2:5],
        group(near_h, 1) + group(near_g, 1)[2:5] + group(near_g, 3)[0:3],
    )
    source = again - restrict_fine((back2[1:13] - back3) * (1.0 / GAIN0))
    source = inside(source, mid - 2, 2 * slabs)

    smoothed = relax(source[1:5], mid_cross)
    coarse_again[slab] = in_rows(restrict_mid(smoothed[0], smoothed[1]))
    for away in (4, -4, 3, -3, 2, -2, 1, -1):
        copy(11, coarse_again.at[slab], coarse_again.at[slab], slab_at(away)).start()

    spill_over.wait_recv()
    spill_pass.start()
    some = coarse_again.at[pl.ds(0, 8)]
    copy(11, some, some, up).wait_recv()
    spill_pass.wait_recv()
    direct += jnp.concatenate([spill_in[0], none], axis=0) + jnp.concatenate([none, spill_in[1]], axis=0)
    padded[pl.ds(3, slabs)] = coarse_solve(coarse_again[...])
    lifted = prolong_mid(padded[pl.ds(slab + 2, 3)])
    guess = GAIN1 * source + lifted
    error = inside(relax(guess, mid_cross) + GAIN1 * source[1:5], mid - 1, 2 * slabs)
    fine[...] = direct + relax(prolong_fine(error)[1:7], fine_cross)
    for c in range(blocks):
        pot_ref[:, c * 128 : (c + 1) * 128] = fine[:, c, :]

    copy(10, kin_in.at[pl.ds(0, blocks - 1)], kin_in.at[pl.ds(0, blocks - 1)], down_cut).wait_recv()
    kin_ref[...] = jnp.sum(kin_in[...], axis=0)

    copy(0, dens_in.at[pl.ds(0, blocks - 1)], dens_in.at[pl.ds(0, blocks - 1)], down_cut).wait_send()
    for k in range(2):
        for rim in rim_copies(k):
            rim.wait_send()
    copy(3, gathered, gathered, down_cut).wait_send()
    spill_over.wait_send()
    spill_pass.wait_send()
    copy(6, all_but_one, all_but_one, up).wait_send()
    copy(7, near.at[pl.ds(0, 6)], near.at[pl.ds(0, 6)], up).wait_send()
    copy(8, arrived, arrived, down_cut).wait_send()
    near_pass.wait_send()
    copy(10, kin_in.at[pl.ds(0, blocks - 1)], kin_in.at[pl.ds(0, blocks - 1)], down_cut).wait_send()
    copy(11, some, some, up).wait_send()


def solution(mesh):
    blocks, slabs = mesh.shape["cuts"], mesh.shape["slab"]

    def shards(orbitals, occupation, state_counts, ion_charge):
        f32, bf16 = jnp.float32, jnp.bfloat16
        anywhere, vmem = pl.BlockSpec(memory_space=pl.ANY), pl.BlockSpec(memory_space=pltpu.VMEM)
        return pl.pallas_call(
            functools.partial(kernel, blocks, slabs),
            out_shape=(jax.ShapeDtypeStruct((4, 4096), f32), jax.ShapeDtypeStruct((4, 128), f32)),
            in_specs=[anywhere, anywhere, pl.BlockSpec(memory_space=pltpu.SMEM), anywhere],
            out_specs=(vmem, vmem),
            scratch_shapes=[
                pltpu.VMEM((1, 32), jnp.int32),
                pltpu.VMEM((4, 4096), f32),
                pltpu.VMEM((32, 4, 4096), bf16),
                pltpu.VMEM((32, 4, 128), f32),
                pltpu.VMEM((128, 128), f32),
                pltpu.VMEM((4, 32, 4096), bf16),
                pltpu.VMEM((blocks, 4, 128), f32),
                pltpu.VMEM((blocks, 4, 128), f32),
                pltpu.VMEM((blocks, 4, 128), f32),
                pltpu.VMEM((2, 32, 4096), bf16),
                pltpu.VMEM((blocks, 4, 128), f32),
                pltpu.VMEM((blocks, 4, 128), f32),
                pltpu.VMEM((7, 32, 128), f32),
                pltpu.VMEM((2, 3, 32, 128), f32),
                pltpu.VMEM((2, 32, 128), f32),
                pltpu.VMEM((2, 3, 32, 128), f32),
                pltpu.VMEM((2, 3, 32, 128), f32),
                pltpu.VMEM((slabs, 8, 128), f32),
                pltpu.VMEM((slabs, 8, 128), f32),
                pltpu.VMEM((slabs + 6, 8, 128), f32),
                pltpu.VMEM((4, 32, 128), f32),
                pltpu.SemaphoreType.DMA((3,)),
                pltpu.SemaphoreType.DMA((14,)),
                pltpu.SemaphoreType.DMA((14,)),
            ],
            compiler_params=pltpu.CompilerParams(collective_id=0, has_side_effects=True, vmem_limit_bytes=55_900_000),
        )(orbitals, pltpu.with_memory_space_constraint(occupation, pltpu.HBM), state_counts, pltpu.with_memory_space_constraint(ion_charge, pltpu.HBM))

    return jax.shard_map(
        shards,
        mesh=mesh,
        in_specs=(P("cuts", "slab", None), P("cuts", None), P("cuts"), P("slab", None)),
        out_specs=(P("slab", None), P("slab", "cuts")),
        check_vma=False,
    )
```

```python
import functools

import jax
import jax.numpy as jnp
from jax import lax
from jax.experimental import pallas as pl
from jax.experimental.pallas import tpu as pltpu
from jax.sharding import PartitionSpec as P

MESH = pl.DeviceIdType.MESH
NX = 64
OCC_DEN = 8
OMEGA = 0.8
COUPLING = 4.0
STEP = OMEGA / 6.0
GAIN0, GAIN1, GAIN2 = STEP, 4.0 * STEP, 16.0 * STEP


def iota(shape, axis):
    return lax.broadcasted_iota(jnp.int32, shape, axis)


def fine_cross(v):
    shape = v.shape
    lane, row = iota(shape, 2), iota(shape, 1)
    column = lane & 63
    west = jnp.where(column == 0, 0.0, pltpu.roll(v, 1, 2))
    east = jnp.where(column == 63, 0.0, pltpu.roll(v, 127, 2))
    odd = lane >= 64
    before = jnp.where(row == 0, 0.0, pltpu.roll(v, 1, 1))
    after = jnp.where(row == 31, 0.0, pltpu.roll(v, 31, 1))
    return west + east + pltpu.roll(v + jnp.where(odd, before, after), 64, 2)


def mid_cross(v):
    shape = v.shape
    lane, row = iota(shape, 2), iota(shape, 1)
    along = pltpu.roll(v, 1, 2) + pltpu.roll(v, 127, 2)
    before = jnp.where(row == 0, 0.0, pltpu.roll(v, 1, 1))
    after = jnp.where(row == 31, 0.0, pltpu.roll(v, 31, 1))
    return jnp.where(lane < 32, along + before + after, 0.0)


def relax(v, cross):
    inner = v[1:-1]
    return (1.0 - OMEGA) * inner + STEP * (cross(inner) + v[2:] + v[:-2])


def grow(v, cross):
    n = v.shape[0]
    none = jnp.zeros((1, *v.shape[1:]), jnp.float32)
    both = jnp.concatenate([none, none], axis=0)
    middle = jnp.concatenate([none, (1.0 - OMEGA) * v + STEP * cross(v), none], axis=0)
    return middle + STEP * (jnp.concatenate([both, v], axis=0) + jnp.concatenate([v, both], axis=0))


def widened(v, n):
    none = jnp.zeros((n, *v.shape[1:]), jnp.float32)
    return jnp.concatenate([none, v, none], axis=0)


def packed(planes):
    return sum(pltpu.roll(p, 32 * k, 1) if k else p for k, p in enumerate(planes))


def group(v, k):
    return pltpu.roll(v, (128 - 32 * k) % 128, v.ndim - 1) if k else v


def woven(even, odd):
    n = even.shape[0]
    v = jnp.concatenate([even[:, None], odd[:, None]], axis=1).reshape(2 * n, 32, 128)
    return jnp.where(iota(v.shape, 2) < 32, v, 0.0)


def inside(v, first, planes):
    plane = iota(v.shape, 0) + first
    return jnp.where((plane >= 0) & (plane < planes), v, 0.0)


def exact_dot(v, m):
    m = m.astype(jnp.bfloat16)
    total = None
    for unused in range(3):
        part = v.astype(jnp.bfloat16)
        v = v - part.astype(jnp.float32)
        term = jnp.dot(part, m, preferred_element_type=jnp.float32)
        total = term if total is None else total + term
    return total


def flat_dot(v, m):
    n = v.shape[0]
    return exact_dot(v.reshape(n * v.shape[1], 128), m).reshape(n, v.shape[1], 128)


def restrict_fine(v):
    n = v.shape[0]
    pairs = v.reshape(n // 2, 2, 32, 128)
    lane, x = iota((128, 128), 0), iota((128, 128), 1)
    average = jnp.where(((lane & 63) >> 1) == x, 0.125, 0.0)
    return flat_dot(pairs[:, 0] + pairs[:, 1], average)


def prolong_fine(v):
    n = v.shape[0]
    x, lane = iota((128, 128), 0), iota((128, 128), 1)
    spread = flat_dot(v, jnp.where(((lane & 63) >> 1) == x, 1.0, 0.0))
    return jnp.broadcast_to(spread[:, None], (n, 2, 32, 128)).reshape(2 * n, 32, 128)


def own_group(shape):
    return ((iota(shape, len(shape) - 2) >> 1) & 7) == (iota(shape, len(shape) - 1) >> 4)


def restrict_mid(low, high):
    x, lane = iota((128, 128), 0), iota((128, 128), 1)
    average = jnp.where(((lane & 15) == (x >> 1)) & (x < 32), 0.125, 0.0)
    both = exact_dot(low + high, average)
    both = jnp.where(own_group(both.shape), both, 0.0)
    return jnp.sum(both[:16], axis=0, keepdims=True), jnp.sum(both[16:], axis=0, keepdims=True)


def in_rows(rows):
    at = iota((8, 128), 0)
    tile = jnp.zeros((8, 128), jnp.float32)
    for k, row in enumerate(rows):
        tile = jnp.where(at == k, row, tile)
    return tile


def prolong_mid(v):
    n = v.shape[0]
    rows = jnp.concatenate(
        [jnp.broadcast_to(v[:, 0:1], (n, 16, 128)), jnp.broadcast_to(v[:, 1:2], (n, 16, 128))], axis=1
    )
    rows = jnp.where(own_group(rows.shape), rows, 0.0)
    lane, x = iota((128, 128), 0), iota((128, 128), 1)
    spread = flat_dot(rows, jnp.where(((lane & 15) == (x >> 1)) & (x < 32), 1.0, 0.0))
    return jnp.broadcast_to(spread[:, None], (n, 2, 32, 128)).reshape(2 * n, 32, 128)


def coarse_solve(source):
    shape = source.shape
    lane, row = iota(shape, 2), iota(shape, 1)
    column, group = lane & 15, lane >> 4
    zero = jnp.zeros((1, *shape[1:]), jnp.float32)
    gained = GAIN2 * source
    v = gained
    for unused in range(3):
        west = jnp.where(column == 0, 0.0, pltpu.roll(v, 1, 2))
        east = jnp.where(column == 15, 0.0, pltpu.roll(v, 127, 2))
        back, on = pltpu.roll(v, 16, 2), pltpu.roll(v, 112, 2)
        before = jnp.where(group == 0, pltpu.roll(back, 1, 1), back)
        after = jnp.where(group == 7, pltpu.roll(on, 7, 1), on)
        plane = jnp.where(row < 2, west + east + before + after, 0.0)
        below = jnp.concatenate([zero, v[:-1]], axis=0)
        above = jnp.concatenate([v[1:], zero], axis=0)
        v = (1.0 - OMEGA) * v + STEP * (plane + below + above) + gained
    return v


def far_first(n):
    return sorted(range(n), key=lambda step: -min(step, n - step))


def kernel(
    blocks, slabs,
    orb_ref, occ_ref, count_ref, ion_ref,
    out_ref,
    occ, ion, raw, wide, stage, planar, dens, dens_in, field, rims, kin, kin_in,
    near, low_near, own_near, spill, spill_in, coarse, coarse_again, padded, fine,
    load_sem, send_sem, recv_sem,
):
    me, slab = lax.axis_index("cuts"), lax.axis_index("slab")
    planes = 4 * slabs

    load = pltpu.make_async_copy(orb_ref, raw, load_sem.at[0])
    load_small = pltpu.make_async_copy(occ_ref, occ, load_sem.at[1])
    load_ion = pltpu.make_async_copy(ion_ref, ion, load_sem.at[2])
    load_small.start()
    load.start()
    load_ion.start()

    ring = blocks // 4
    half, y, core = me // (2 * ring), lax.rem(me // 2, ring), lax.rem(me, 2)
    others = [
        (h * ring + lax.rem(y + step, ring)) * 2 + c
        for step in far_first(ring)
        for h in (1 - half, half)
        for c in (1 - core, core)
    ][:-1]

    def cut_at(number):
        return {"cuts": number}

    def slab_at(r):
        return {"slab": lax.rem(slab + r + slabs, slabs)}

    other_slabs = [slab_at(step) for step in far_first(slabs)[:-1]]

    up, down, down_cut = slab_at(1), slab_at(-1), cut_at(others[-1])
    barrier = pltpu.get_barrier_semaphore()

    for device in [cut_at(number) for number in others] + other_slabs:
        pl.semaphore_signal(barrier, inc=1, device_id=device, device_id_type=MESH)

    def copy(stage, src, dst, device):
        return pltpu.make_async_remote_copy(
            src_ref=src, dst_ref=dst, send_sem=send_sem.at[stage], recv_sem=recv_sem.at[stage],
            device_id=device, device_id_type=MESH,
        )

    def columns(c):
        return pl.ds(pl.multiple_of(c * 128, 128), 128)

    coarse_again[...] = jnp.zeros_like(coarse_again)
    load_small.wait()
    square = (32, 32)
    column = jnp.sum(
        jnp.where(
            iota(square, 0) == iota(square, 1),
            jnp.broadcast_to(occ[...].astype(jnp.float32), square), 0.0,
        ),
        axis=1, keepdims=True,
    ) * (1.0 / OCC_DEN)
    live = iota((32, 128), 0) < count_ref[0]
    weight = jnp.where(live, jnp.broadcast_to(column, (32, 128)), 0.0)
    wide[...] = jnp.broadcast_to(weight[:, None], (32, 4, 128))
    load.wait()

    @pl.loop(0, blocks)
    def _(c):
        p = raw[:, :, columns(c)].astype(jnp.float32)
        dens[c] = jnp.sum(wide[...] * (p * p), axis=0)

    pl.semaphore_wait(barrier, blocks + slabs - 2)

    for k, number in enumerate(others):
        copy(0, dens.at[number], dens_in.at[k], cut_at(number)).start()

    dens_in[blocks - 1] = dens[me]

    @pl.loop(0, blocks)
    def _(c):
        stage[...] = raw[:, :, columns(c)].astype(jnp.float32).reshape(128, 128)
        for z in range(4):
            planar[z, :, columns(c)] = stage[pl.ds(z, 32, stride=4), :].astype(jnp.bfloat16)

    def rim_copies(k):
        part = pl.ds(2048 * k, 2048)
        return (
            copy(1 + k, planar.at[3, :, part], rims.at[0, :, part], up),
            copy(12 + k, planar.at[0, :, part], rims.at[1, :, part], down),
        )

    for rim in rim_copies(0):
        rim.start()

    lane = iota((32, 128), 1)
    x = lane & 63
    odd = lane >= 64

    def tile(z, c):
        return planar[z, :, columns(c)].astype(jnp.float32)

    def folded(v):
        return (v[:8] + v[8:16]) + (v[16:24] + v[24:])

    def plain_terms(c):
        left = jnp.where(c > 0, 1.0, 0.0)
        right = jnp.where(c < blocks - 1, 1.0, 0.0)
        ps = [tile(z, c) for z in range(4)]
        rows = []
        for z in range(4):
            p = ps[z]
            along = jnp.where(x == 0, 0.0, p) - jnp.where(x == 1, 0.0, pltpu.roll(p, 2, 1))
            total = pltpu.roll(folded(weight * (along * along)), 127, 1)
            back = p - left * tile(z, lax.max(c - 1, 0))
            on = right * tile(z, lax.min(c + 1, blocks - 1)) - p
            across = jnp.where(odd, back, on)
            total += pltpu.roll(folded(weight * (across * across)), 64, 1)
            if z in (1, 2):
                steep = ps[z + 1] - ps[z - 1]
                total += folded(weight * (steep * steep))
            rows.append(jnp.sum(total, axis=0, keepdims=True) * 0.125)
        kin[c] = jnp.concatenate(rows, axis=0)

    early = 3 * blocks // 8
    pl.loop(0, early)(plain_terms)

    copy(0, dens_in.at[pl.ds(0, blocks - 1)], dens_in.at[pl.ds(0, blocks - 1)], down_cut).wait_recv()
    load_ion.wait()
    field[me] = COUPLING * (jnp.sum(dens_in[...], axis=0) - ion[:, columns(me)])

    for number in others:
        copy(3, field.at[me], field.at[me], cut_at(number)).start()

    for rim in rim_copies(1):
        rim.start()

    pl.loop(early, blocks)(plain_terms)

    gathered = field.at[pl.ds(0, blocks - 1)]
    copy(3, gathered, gathered, down_cut).wait_recv()

    for z in range(4):
        fine[z] = field[:, z, :]
    first, mid = 4 * slab, 2 * slab
    forcing = fine[...]
    left1 = inside(grow(forcing, fine_cross), first - 1, planes)
    source = restrict_fine(widened(left1, 1))
    near[6] = packed([source[k] for k in range(4)])
    for k, away in enumerate((3, -3, 2, -2, 1, -1)):
        copy(7, near.at[6], near.at[k], slab_at(away)).start()
    below = inside(grow(source, mid_cross), mid - 2, 2 * slabs)
    coarse[slab] = in_rows([row for k in range(3) for row in restrict_mid(below[2 * k], below[2 * k + 1])])

    for device in other_slabs:
        copy(6, coarse.at[slab], coarse.at[slab], device).start()

    left2 = inside(grow(left1, fine_cross), first - 2, planes)
    left3 = inside(grow(left2, fine_cross), first - 3, planes)
    again = restrict_fine(widened(left3, 1))
    own_near[0] = packed([again[0], again[1], again[4], again[5]])
    own_near[1] = packed([again[2], again[3]])
    toward = 1 - 2 * core
    for k, (block, steps) in enumerate(((0, 1), (0, 2), (1, 1))):
        copy(8, own_near.at[block], low_near.at[core, k], slab_at(steps * toward)).start()
    direct = GAIN0 * (left3 + widened(left2, 1) + widened(left1, 2) + widened(forcing, 3))
    spill[0] = direct[:3]
    spill[1] = direct[7:]
    direct = direct[3:7]
    spill_over = copy(4, spill.at[1 - core], spill_in.at[core], slab_at(toward))
    spill_over.start()
    spill_pass = copy(5, spill_in.at[core], spill_in.at[core], down_cut)

    for k in range(2):
        for rim in rim_copies(k):
            rim.wait_recv()
    has_below = jnp.where(slab > 0, 1.0, 0.0)
    has_above = jnp.where(slab < slabs - 1, 1.0, 0.0)
    row4 = iota((4, 128), 0)

    @pl.loop(0, blocks)
    def _(c):
        low = tile(1, c) - has_below * rims[0, :, columns(c)].astype(jnp.float32)
        high = has_above * rims[1, :, columns(c)].astype(jnp.float32) - tile(2, c)
        low = jnp.sum(weight * (low * low), axis=0, keepdims=True) * 0.125
        high = jnp.sum(weight * (high * high), axis=0, keepdims=True) * 0.125
        kin[c] += jnp.where(row4 == 0, low, jnp.where(row4 == 3, high, 0.0))

    for k, number in enumerate(others):
        copy(10, kin.at[number], kin_in.at[k], cut_at(number)).start()

    kin_in[blocks - 1] = kin[me]

    all_but_one = coarse.at[pl.ds(0, slabs - 1)]
    copy(6, all_but_one, all_but_one, up).wait_recv()
    arrived = low_near.at[core]
    copy(8, arrived, arrived, down_cut).wait_recv()
    near_pass = copy(9, arrived, arrived, down_cut)
    near_pass.start()
    parts = coarse[...]
    none = jnp.zeros((1, 8, 128), jnp.float32)
    parts = (
        pltpu.roll(parts, 6, 1)
        + jnp.concatenate([none, pltpu.roll(parts, 4, 1)[:-1]], axis=0)
        + jnp.concatenate([parts[1:], none], axis=0)
    )
    padded[pl.ds(0, 3)] = jnp.zeros((3, 8, 128), jnp.float32)
    padded[pl.ds(slabs + 3, 3)] = jnp.zeros((3, 8, 128), jnp.float32)
    padded[pl.ds(3, slabs)] = coarse_solve(jnp.where(iota(parts.shape, 1) < 2, parts, 0.0))
    lifted = prolong_mid(padded[pl.ds(slab, 7)])
    copy(7, near.at[pl.ds(0, 6)], near.at[pl.ds(0, 6)], up).wait_recv()
    near_f = jnp.stack([near[0], near[2], near[4], near[6], near[5], near[3], near[1]])
    near_f = inside(near_f, slab - 3, slabs)
    none = jnp.zeros((1, 32, 128), jnp.float32)
    source = woven(
        group(near_f, 1) + jnp.concatenate([none, group(near_f, 3)[:-1]], axis=0),
        group(near_f, 2) + jnp.concatenate([near_f[1:], none], axis=0),
    )
    source = inside(source, mid - 6, 2 * slabs)
    guess = GAIN1 * source[1:13] + lifted[1:13]
    error = inside(relax(guess, mid_cross) + GAIN1 * source[2:12], mid - 4, 2 * slabs)
    spread = prolong_fine(error)[1:19]
    back1 = inside(relax(spread, fine_cross), first - 6, planes)
    back2 = inside(relax(back1, fine_cross), first - 5, planes)
    back3 = relax(back2, fine_cross)
    direct += back3[4:8]
    near_pass.wait_recv()
    near_g = jnp.stack([low_near[0, 1], low_near[0, 0], own_near[0], low_near[1, 0], low_near[1, 1]])
    near_g = inside(near_g, slab - 2, slabs)
    near_h = jnp.stack([low_near[0, 2], own_near[1], low_near[1, 2]])
    again = woven(
        near_h + group(near_g, 2)[0:3] + near_g[2:5],
        group(near_h, 1) + group(near_g, 1)[2:5] + group(near_g, 3)[0:3],
    )
    source = again - restrict_fine((back2[1:13] - back3) * (1.0 / GAIN0))
    source = inside(source, mid - 2, 2 * slabs)

    smoothed = relax(source[1:5], mid_cross)
    coarse_again[slab] = in_rows(restrict_mid(smoothed[0], smoothed[1]))
    for away in (4, -4, 3, -3, 2, -2, 1, -1):
        copy(11, coarse_again.at[slab], coarse_again.at[slab], slab_at(away)).start()

    spill_over.wait_recv()
    spill_pass.start()
    some = coarse_again.at[pl.ds(0, 8)]
    copy(11, some, some, up).wait_recv()
    spill_pass.wait_recv()
    direct += jnp.concatenate([spill_in[0], none], axis=0) + jnp.concatenate([none, spill_in[1]], axis=0)
    padded[pl.ds(3, slabs)] = coarse_solve(coarse_again[...])
    lifted = prolong_mid(padded[pl.ds(slab + 2, 3)])
    guess = GAIN1 * source + lifted
    error = inside(relax(guess, mid_cross) + GAIN1 * source[1:5], mid - 1, 2 * slabs)
    fine[...] = direct + relax(prolong_fine(error)[1:7], fine_cross)
    for c in range(blocks):
        out_ref[:, c * 128 : (c + 1) * 128] = fine[:, c, :]

    copy(10, kin_in.at[pl.ds(0, blocks - 1)], kin_in.at[pl.ds(0, blocks - 1)], down_cut).wait_recv()
    out_ref[:, 4096:] = jnp.sum(kin_in[...], axis=0)

    copy(0, dens_in.at[pl.ds(0, blocks - 1)], dens_in.at[pl.ds(0, blocks - 1)], down_cut).wait_send()
    for k in range(2):
        for rim in rim_copies(k):
            rim.wait_send()
    copy(3, gathered, gathered, down_cut).wait_send()
    spill_over.wait_send()
    spill_pass.wait_send()
    copy(6, all_but_one, all_but_one, up).wait_send()
    copy(7, near.at[pl.ds(0, 6)], near.at[pl.ds(0, 6)], up).wait_send()
    copy(8, arrived, arrived, down_cut).wait_send()
    near_pass.wait_send()
    copy(10, kin_in.at[pl.ds(0, blocks - 1)], kin_in.at[pl.ds(0, blocks - 1)], down_cut).wait_send()
    copy(11, some, some, up).wait_send()


def solution(mesh):
    blocks, slabs = mesh.shape["cuts"], mesh.shape["slab"]

    def shards(orbitals, occupation, state_counts, ion_charge):
        f32, bf16 = jnp.float32, jnp.bfloat16
        anywhere, vmem = pl.BlockSpec(memory_space=pl.ANY), pl.BlockSpec(memory_space=pltpu.VMEM)
        both = pl.pallas_call(
            functools.partial(kernel, blocks, slabs),
            out_shape=jax.ShapeDtypeStruct((4, 4224), f32),
            in_specs=[anywhere, anywhere, pl.BlockSpec(memory_space=pltpu.SMEM), anywhere],
            out_specs=vmem,
            scratch_shapes=[
                pltpu.VMEM((1, 32), jnp.int32),
                pltpu.VMEM((4, 4096), f32),
                pltpu.VMEM((32, 4, 4096), bf16),
                pltpu.VMEM((32, 4, 128), f32),
                pltpu.VMEM((128, 128), f32),
                pltpu.VMEM((4, 32, 4096), bf16),
                pltpu.VMEM((blocks, 4, 128), f32),
                pltpu.VMEM((blocks, 4, 128), f32),
                pltpu.VMEM((blocks, 4, 128), f32),
                pltpu.VMEM((2, 32, 4096), bf16),
                pltpu.VMEM((blocks, 4, 128), f32),
                pltpu.VMEM((blocks, 4, 128), f32),
                pltpu.VMEM((7, 32, 128), f32),
                pltpu.VMEM((2, 3, 32, 128), f32),
                pltpu.VMEM((2, 32, 128), f32),
                pltpu.VMEM((2, 3, 32, 128), f32),
                pltpu.VMEM((2, 3, 32, 128), f32),
                pltpu.VMEM((slabs, 8, 128), f32),
                pltpu.VMEM((slabs, 8, 128), f32),
                pltpu.VMEM((slabs + 6, 8, 128), f32),
                pltpu.VMEM((4, 32, 128), f32),
                pltpu.SemaphoreType.DMA((3,)),
                pltpu.SemaphoreType.DMA((14,)),
                pltpu.SemaphoreType.DMA((14,)),
            ],
            compiler_params=pltpu.CompilerParams(collective_id=0, has_side_effects=True, vmem_limit_bytes=55_900_000),
        )(orbitals, pltpu.with_memory_space_constraint(occupation, pltpu.HBM), state_counts, pltpu.with_memory_space_constraint(ion_charge, pltpu.HBM))
        return both[:, :4096], both[:, 4096:]

    return jax.shard_map(
        shards,
        mesh=mesh,
        in_specs=(P("cuts", "slab", None), P("cuts", None), P("cuts"), P("slab", None)),
        out_specs=(P("slab", None), P("slab", "cuts")),
        check_vma=False,
    )
```
